128 devices in a mesh: dom: 128 (over x, z, y, core).
Axes of the slice: x: 4, y: 4, z: 4, core: 2. Of those that a mesh axis runs over, the one named last changes fastest.
Arguments:
- features: bfloat16 [262144, 512], P('dom'), may hold values from -6 to 6
- weight: bfloat16 [512, 512], replicated, may hold values from -0.25 to 0.25
- cotangent: bfloat16 [262144, 512], P('dom'), may hold values from -6 to 6
- tile_values: bfloat16 [12288, 128, 128], P('dom'), may hold values from -0.21875 to 0.21875
- tile_rows: int32 [12288], P('dom'), may hold values from 0 to 15
- tile_cols: int32 [12288], P('dom'), may hold values from 0 to 27, as said below
- hub_rows: int32 [512], P('dom'), may hold values from 0 to 2047
- send_rows: int32 [128, 128, 8], P('dom'), may hold values from 0 to 2047
- send_count: int32 [128, 128], P('dom'), may hold values from 1 to 8, as said below
Outputs:
- output: bfloat16 [262144, 512], P('dom')
- grad_features: bfloat16 [262144, 512], P('dom')
- grad_weight: float32 [512, 512], replicated
The draws below stay inside these ranges and needn't reach their ends.
Inputs may be any that keep to these rules, and one draw needn't show every extreme that they name: `tile_cols`: on every device the first 64 tiles name column blocks below 20 and the other 32 name blocks from 20 on. `send_count`: every source sends 8 rows to at least one device.
All inputs are finite; a program needn't handle non-finite values.
Results may differ from the reference program's by a relative error of at most 0.019.
Values may be sent and summed in bfloat16 or wider, within the bound.
A program may use at most 128 MiB of HBM per device.

```python
import jax
import jax.numpy as jnp
from jax import lax

F = 512
TILE = 128
R_DEV = 2048
LOC_TILES = 64
HALO_TILES = 32
HUBS_DEV = 4
SLOTS = 8
TILES_DEV = 96
VERTICES = 262144
TILES = 12288
HUBS = 512
ROW_BLOCKS = 16
LOC_BLOCKS = 20
EXT_BLOCKS = 28
N_DOM = 128


def draw_tile_cols(key, part):
    key_near, key_far, key_pick = jax.random.split(key, 3)
    near = jax.random.randint(key_near, (N_DOM, LOC_TILES), 0, LOC_BLOCKS)
    far = jax.random.randint(key_far, (N_DOM, HALO_TILES), LOC_BLOCKS, EXT_BLOCKS)
    chosen = jax.random.randint(key_pick, (), 0, N_DOM)
    near = near.at[chosen, 0].set(0)
    far = far.at[chosen, HALO_TILES - 1].set(EXT_BLOCKS - 1)
    return jnp.concatenate([near, far], axis=1).reshape(-1).astype(jnp.int32)


def draw_send_count(key, part):
    key_count, key_offset = jax.random.split(key, 2)
    counts = jax.random.randint(key_count, (N_DOM, N_DOM), 1, SLOTS + 1)
    offset = jax.random.randint(key_offset, (N_DOM,), 0, N_DOM)
    senders = jnp.arange(N_DOM, dtype=jnp.int32)
    filled = senders[None, :] == ((senders + offset) % N_DOM)[:, None]
    return jnp.where(filled, SLOTS, counts).astype(jnp.int32)


def with_ends(array, stream_key, smallest, top_value):
    longest = array.shape.index(max(array.shape))
    spots = []
    for shift in (0, 1):
        where = [jax.random.randint(jax.random.fold_in(stream_key, axis), (), 0, length) for axis, length in enumerate(array.shape)]
        where[longest] = (where[longest] + shift) % array.shape[longest]
        spots.append(tuple(where))
    return array.at[spots[0]].set(smallest).at[spots[1]].set(top_value)


def block_levels(own_key, dims, shards, smallest, largest):
    loudness, own = 1.0, jax.random.fold_in(own_key, 6)
    for axis_at, shards_of in shards:
        heights = jnp.exp(jax.random.uniform(jax.random.fold_in(own, axis_at), (shards_of,), jnp.float32, smallest / len(shards), largest / len(shards)))
        loudness = loudness * jnp.repeat(heights, dims[axis_at] // shards_of).reshape([-1 if axis == axis_at else 1 for axis in range(len(dims))])
    return loudness


def noise(key, extent, spread, reach, shards=(), kind=jnp.bfloat16):
    entries = spread * jax.random.normal(key, extent, jnp.float32)
    if shards:
        entries = entries * block_levels(key, extent, shards, -0.22, 0.18)
    return jnp.clip(entries, -reach, reach).astype(kind)


def setup_inputs(seed: int = 0) -> dict:
    streams_of = jax.random.split(jax.random.key(seed), 10)
    features = noise(streams_of[0], (VERTICES, F), 1.0, 6.0, ((0, 128),))
    weight = noise(streams_of[1], (F, F), F ** -0.5, 0.25)
    cotangent = noise(streams_of[2], (VERTICES, F), 1.0, 6.0, ((0, 128),))
    tile_values = noise(streams_of[3], (TILES, TILE, TILE), (TILES_DEV * TILE * TILE // R_DEV) ** -0.5, 0.21875, ((0, 128),))
    tile_rows = with_ends(jax.random.randint(streams_of[4], (TILES,), 0, ROW_BLOCKS), jax.random.fold_in(streams_of[4], 1), 0, ROW_BLOCKS - 1).astype(jnp.int32)
    tile_cols = draw_tile_cols(jax.random.fold_in(streams_of[9], 71), 0)
    hub_rows = with_ends(jax.random.randint(streams_of[6], (HUBS,), 0, R_DEV), jax.random.fold_in(streams_of[6], 1), 0, R_DEV - 1).astype(jnp.int32)
    send_rows = with_ends(jax.random.randint(streams_of[7], (N_DOM, N_DOM, SLOTS), 0, R_DEV), jax.random.fold_in(streams_of[7], 1), 0, R_DEV - 1).astype(jnp.int32)
    send_count = draw_send_count(jax.random.fold_in(streams_of[9], 71), 0)
    return {"features": features, "weight": weight, "cotangent": cotangent, "tile_values": tile_values, "tile_rows": tile_rows, "tile_cols": tile_cols, "hub_rows": hub_rows, "send_rows": send_rows, "send_count": send_count}


def reference(features, weight, cotangent, tile_values, tile_rows, tile_cols, hub_rows, send_rows, send_count):
    bases = jnp.arange(N_DOM, dtype=jnp.int32) * R_DEV
    hub_global = (hub_rows.reshape(N_DOM, HUBS_DEV) + bases[:, None]).reshape(-1)
    slot_ids = jnp.arange(SLOTS, dtype=jnp.int32)

    def aggregate(feat_full):
        hub_all = feat_full[hub_global]

        def one_device(device):
            own_rows = lax.dynamic_slice_in_dim(feat_full, (device * R_DEV).astype(jnp.int32), R_DEV, 0)
            sources = send_rows[:, device, :] + bases[:, None]
            live_slots = slot_ids[None, :] < send_count[:, device][:, None]
            incoming = jnp.where(live_slots.reshape(-1)[:, None], feat_full[sources.reshape(-1)], jnp.zeros((), feat_full.dtype))
            table = jnp.concatenate([own_rows, hub_all, incoming], axis=0).reshape(EXT_BLOCKS, TILE, F)
            start = (device * TILES_DEV).astype(jnp.int32)
            values = lax.dynamic_slice_in_dim(tile_values, start, TILES_DEV, 0).astype(jnp.float32)
            rows_here = lax.dynamic_slice_in_dim(tile_rows, start, TILES_DEV, 0)
            cols_here = lax.dynamic_slice_in_dim(tile_cols, start, TILES_DEV, 0)
            products = jnp.einsum('kij,kjf->kif', values, table[cols_here], precision=lax.Precision.HIGHEST)
            summed = jnp.zeros((ROW_BLOCKS, TILE, F), feat_full.dtype).at[rows_here].add(products)
            return summed.reshape(R_DEV, F)
        return lax.map(one_device, jnp.arange(N_DOM, dtype=jnp.int32)).reshape(-1, F)
    agg_full, pullback = jax.vjp(aggregate, features.astype(jnp.float32))
    aggregated = agg_full.astype(jnp.bfloat16)
    pre_act = jnp.dot(aggregated, weight, preferred_element_type=jnp.float32)
    sigmoid_pre = jax.nn.sigmoid(pre_act)
    output = (pre_act * sigmoid_pre).astype(jnp.bfloat16)
    grad_pre = (cotangent.astype(jnp.float32) * sigmoid_pre * (1.0 + pre_act * (1.0 - sigmoid_pre))).astype(jnp.bfloat16)
    grad_weight = jnp.dot(aggregated.T, grad_pre, preferred_element_type=jnp.float32) * float(VERTICES) ** (-0.5)
    grad_agg = jnp.dot(grad_pre, weight.T, preferred_element_type=jnp.float32).astype(jnp.bfloat16)
    grad_features = pullback(grad_agg.astype(jnp.float32))[0].astype(jnp.bfloat16)
    return (output, grad_features, grad_weight)
```

```python
import functools

import jax
import jax.numpy as jnp
from jax import lax
from jax.experimental import pallas as pl
from jax.experimental.pallas import tpu as pltpu
from jax.sharding import PartitionSpec as P

MESH = pl.DeviceIdType.MESH
N = 128
F = 512
R = 2048
TILE = 128
SLOTS = 8
HUBS = 4
TILES = 96
F32 = jnp.float32
BF16 = jnp.bfloat16
VMEM_SPEC = pl.BlockSpec(memory_space=pltpu.VMEM)
ANY_SPEC = pl.BlockSpec(memory_space=pl.ANY)
SMEM_SPEC = pl.BlockSpec(memory_space=pltpu.SMEM)
LIMIT = 60 * 1024 * 1024


def peer_of(me, i):
    return lax.rem(me + i, N)


def greet():
    me = lax.axis_index("dom")
    barrier = pltpu.get_barrier_semaphore()

    @pl.loop(1, N)
    def _(i):
        pl.semaphore_signal(barrier, inc=1, device_id=(peer_of(me, i),), device_id_type=MESH)

    return barrier


def meet(barrier):
    pl.semaphore_wait(barrier, N - 1)


def whole_wait(ref, sem):
    pltpu.make_async_copy(ref, ref, sem).wait()


def halo_send(idx_ref, hub_idx_ref, feat_ref, far_ref, hub_ref, out_buf, hub_buf, send, recv):
    me = lax.axis_index("dom")
    barrier = greet()
    feats = feat_ref[...]
    lanes = lax.broadcasted_iota(jnp.int32, (TILE, R), 1)
    for b in range(N * SLOTS // TILE):
        picks = (idx_ref[pl.ds(b * TILE, TILE), :] == lanes).astype(F32).astype(BF16)
        rows = jnp.dot(picks, feats, preferred_element_type=F32)
        out_buf[pl.ds(b * 16, 16)] = rows.reshape(16, SLOTS, F).astype(BF16)
    picks = (hub_idx_ref[...] == lanes[:8]).astype(F32).astype(BF16)
    rows = jnp.dot(picks, feats, preferred_element_type=F32)
    hub_buf[0] = rows[:HUBS].astype(BF16)
    meet(barrier)
    own = (
        pltpu.make_async_copy(out_buf.at[me], far_ref.at[me], recv.at[0]),
        pltpu.make_async_copy(hub_buf.at[0], hub_ref.at[me], recv.at[1]),
    )
    for copy in own:
        copy.start()

    @pl.loop(1, N)
    def _(i):
        peer = peer_of(me, i)
        pltpu.make_async_remote_copy(
            src_ref=out_buf.at[peer], dst_ref=far_ref.at[me], send_sem=send.at[0],
            recv_sem=recv.at[0], device_id=(peer,), device_id_type=MESH,
        ).start()
        pltpu.make_async_remote_copy(
            src_ref=hub_buf.at[0], dst_ref=hub_ref.at[me], send_sem=send.at[1],
            recv_sem=recv.at[1], device_id=(peer,), device_id_type=MESH,
        ).start()

    whole_wait(out_buf.at[pl.ds(0, N - 1)], send.at[0])
    whole_wait(hub_ref.at[pl.ds(0, N - 1)], send.at[1])
    whole_wait(far_ref, recv.at[0])
    whole_wait(hub_ref, recv.at[1])


def call_halo_send(idx, hub_idx, features):
    return pl.pallas_call(
        halo_send,
        out_shape=(
            jax.ShapeDtypeStruct((N, SLOTS, F), BF16),
            jax.ShapeDtypeStruct((N, HUBS, F), BF16),
        ),
        in_specs=[VMEM_SPEC] * 3,
        out_specs=(ANY_SPEC, ANY_SPEC),
        scratch_shapes=[
            pltpu.VMEM((N, SLOTS, F), BF16),
            pltpu.VMEM((1, HUBS, F), BF16),
            pltpu.SemaphoreType.DMA((2,)),
            pltpu.SemaphoreType.DMA((2,)),
        ],
        compiler_params=pltpu.CompilerParams(
            collective_id=0, has_side_effects=True, vmem_limit_bytes=LIMIT
        ),
        name="halo_send",
    )(idx, hub_idx, features)


def layer(
    rows_ref, cols_ref, tiles_ref, feat_ref, hub_ref, far_ref, cot_ref, weight_ref,
    out_ref, own_ref, hub_grad_ref, far_grad_ref, term_ref,
    tiles, table, cot, acc, grads, gagg, term, sems,
):
    loads = (
        pltpu.make_async_copy(tiles_ref, tiles, sems.at[0]),
        pltpu.make_async_copy(feat_ref, table.at[pl.ds(0, 16)], sems.at[1]),
        pltpu.make_async_copy(hub_ref, table.at[pl.ds(16, 4)], sems.at[2]),
        pltpu.make_async_copy(far_ref, table.at[pl.ds(20, 8)], sems.at[3]),
        pltpu.make_async_copy(cot_ref, cot, sems.at[4]),
    )
    for copy in loads:
        copy.start()
    acc[...] = jnp.zeros_like(acc)
    for copy in loads[:4]:
        copy.wait()

    @pl.loop(0, TILES // 4)
    def _(k):
        for u in range(4):
            t = 4 * k + u
            acc[rows_ref[t]] += jnp.dot(
                tiles[t], table[cols_ref[t]], preferred_element_type=F32
            )

    loads[4].wait()
    term[...] = jnp.zeros_like(term)
    weight = weight_ref[...]

    @pl.loop(0, 8)
    def _(k):
        agg = acc[pl.ds(2 * k, 2)].reshape(256, F).astype(BF16)
        pre = jnp.dot(agg, weight, preferred_element_type=F32)
        sig = 0.5 * jnp.tanh(0.5 * pre) + 0.5
        here = pl.ds(pl.multiple_of(k * 256, 256), 256)
        out_ref[here, :] = (pre * sig).astype(BF16)
        gpre = (cot[here, :].astype(F32) * sig * (1.0 + pre * (1.0 - sig))).astype(BF16)
        term[...] += lax.dot_general(
            agg, gpre, (((0,), (0,)), ((), ())), preferred_element_type=F32
        )
        back = lax.dot_general(gpre, weight, (((1,), (1,)), ((), ())), preferred_element_type=F32)
        gagg[pl.ds(2 * k, 2)] = back.astype(BF16).reshape(2, TILE, F)

    term_ref[...] = (term[...] * (1.0 / 512.0)).astype(BF16)
    grads[...] = jnp.zeros_like(grads)

    @pl.loop(0, TILES // 4)
    def _(k):
        for u in range(4):
            t = 4 * k + u
            grads[cols_ref[t]] += lax.dot_general(
                tiles[t], gagg[rows_ref[t]], (((0,), (0,)), ((), ())), preferred_element_type=F32
            )

    own_ref[...] = grads[pl.ds(0, 16)]
    hub_grad_ref[...] = grads[pl.ds(16, 4)].astype(BF16)
    far_grad_ref[...] = grads[pl.ds(20, 8)].astype(BF16)


def call_layer(rows, cols, tiles, feats, hubs, far, cot, weight):
    return pl.pallas_call(
        layer,
        out_shape=(
            jax.ShapeDtypeStruct((R, F), BF16),
            jax.ShapeDtypeStruct((16, TILE, F), F32),
            jax.ShapeDtypeStruct((4, TILE, F), BF16),
            jax.ShapeDtypeStruct((8, TILE, F), BF16),
            jax.ShapeDtypeStruct((F, F), BF16),
        ),
        in_specs=[SMEM_SPEC] * 2 + [ANY_SPEC] * 5 + [VMEM_SPEC],
        out_specs=(VMEM_SPEC,) * 5,
        scratch_shapes=[
            pltpu.VMEM((TILES, TILE, TILE), BF16),
            pltpu.VMEM((28, TILE, F), BF16),
            pltpu.VMEM((R, F), BF16),
            pltpu.VMEM((16, TILE, F), F32),
            pltpu.VMEM((28, TILE, F), F32),
            pltpu.VMEM((16, TILE, F), BF16),
            pltpu.VMEM((F, F), F32),
            pltpu.SemaphoreType.DMA((5,)),
        ],
        compiler_params=pltpu.CompilerParams(vmem_limit_bytes=LIMIT),
        name="layer",
    )(rows, cols, tiles, feats, hubs, far, cot, weight)


def grad_return(
    idx_ref, hub_idx_ref, far_ref, hub_ref, term_ref, own_ref,
    out_ref, weight_ref,
    far_in, hub_in, term_in, share, gathered, picks, send, recv,
):
    me = lax.axis_index("dom")
    barrier = greet()
    rows = lax.broadcasted_iota(jnp.int32, (TILE, N * SLOTS), 0)

    @pl.loop(0, 16)
    def _(k):
        here = pl.ds(pl.multiple_of(k * TILE, TILE), TILE)
        picks[here, :] = (idx_ref[...] == rows + k * TILE).astype(F32).astype(BF16)

    meet(barrier)
    pltpu.make_async_copy(term_ref.at[me], term_in.at[me], recv.at[0]).start()
    pltpu.make_async_copy(hub_ref.at[me], hub_in.at[me], recv.at[1]).start()
    pltpu.make_async_copy(far_ref.at[me], far_in.at[me], recv.at[2]).start()

    for s, (src, dst) in enumerate(((term_ref, term_in), (hub_ref, hub_in), (far_ref, far_in))):
        @pl.loop(1, N)
        def _(i):
            peer = peer_of(me, i)
            pltpu.make_async_remote_copy(
                src_ref=src.at[peer], dst_ref=dst.at[me], send_sem=send.at[s],
                recv_sem=recv.at[s], device_id=(peer,), device_id_type=MESH,
            ).start()

    whole_wait(term_in, recv.at[0])
    share[0] = jnp.sum(term_in[...].astype(F32), axis=0).astype(BF16)
    pltpu.make_async_copy(share.at[0], gathered.at[me], recv.at[3]).start()

    @pl.loop(1, N)
    def _(i):
        peer = peer_of(me, i)
        pltpu.make_async_remote_copy(
            src_ref=share.at[0], dst_ref=gathered.at[me], send_sem=send.at[3],
            recv_sem=recv.at[3], device_id=(peer,), device_id_type=MESH,
        ).start()

    whole_wait(hub_in, recv.at[1])
    hub_sum = jnp.sum(hub_in[...].astype(F32), axis=0)
    whole_wait(far_in, recv.at[2])
    returned = far_in[...].reshape(N * SLOTS, F)

    lane_rows = lax.broadcasted_iota(jnp.int32, (TILE, F), 0)

    @pl.loop(0, 16)
    def _(k):
        here = pl.ds(pl.multiple_of(k * TILE, TILE), TILE)
        total = own_ref[here, :] + jnp.dot(picks[here, :], returned, preferred_element_type=F32)
        for j in range(HUBS):
            mine = lane_rows + k * TILE == hub_idx_ref[j]
            total += jnp.where(mine, hub_sum[j : j + 1, :], 0.0)
        out_ref[here, :] = total.astype(BF16)

    whole_wait(gathered, recv.at[3])
    weight_ref[...] = gathered[...].astype(F32)
    for s, ref in enumerate((term_in, hub_in, far_in, gathered)):
        whole_wait(ref.at[pl.ds(0, N - 1)], send.at[s])


def call_grad_return(idx, hub_idx, far, hub, term, own):
    return pl.pallas_call(
        grad_return,
        out_shape=(
            jax.ShapeDtypeStruct((R, F), BF16),
            jax.ShapeDtypeStruct((N, 4, F), F32),
        ),
        in_specs=[VMEM_SPEC, SMEM_SPEC] + [VMEM_SPEC] * 4,
        out_specs=(VMEM_SPEC, VMEM_SPEC),
        scratch_shapes=[
            pltpu.VMEM((N, SLOTS, F), BF16),
            pltpu.VMEM((N, HUBS, F), BF16),
            pltpu.VMEM((N, 4, F), BF16),
            pltpu.VMEM((1, 4, F), BF16),
            pltpu.VMEM((N, 4, F), BF16),
            pltpu.VMEM((R, N * SLOTS), BF16),
            pltpu.SemaphoreType.DMA((4,)),
            pltpu.SemaphoreType.DMA((4,)),
        ],
        compiler_params=pltpu.CompilerParams(
            collective_id=1, has_side_effects=True, vmem_limit_bytes=LIMIT
        ),
        name="grad_return",
    )(idx, hub_idx, far, hub, term, own)


def per_device(
    features, weight, cotangent, tile_values, tile_rows, tile_cols, hub_rows, send_rows, send_count
):
    live = jnp.arange(SLOTS, dtype=jnp.int32)[None, :] < send_count[0][:, None]
    idx = jnp.where(live, send_rows[0], -1)
    hub_col = jnp.concatenate([hub_rows, jnp.full((4,), -1, jnp.int32)]).reshape(8, 1)
    far, hub = call_halo_send(idx.reshape(N * SLOTS, 1), hub_col, features)
    output, own, hub_grad, far_grad, term = call_layer(
        tile_rows, tile_cols, tile_values, features.reshape(16, TILE, F),
        hub.reshape(4, TILE, F), far.reshape(8, TILE, F), cotangent, weight,
    )
    grad_features, grad_weight = call_grad_return(
        idx.reshape(1, N * SLOTS), hub_rows, far_grad.reshape(N, SLOTS, F),
        hub_grad.reshape(N, HUBS, F), term.reshape(N, 4, F), own.reshape(R, F),
    )
    return output, grad_features, grad_weight.reshape(F, F)


def solution(mesh):
    placed = (
        P("dom", None),
        P(),
        P("dom", None),
        P("dom", None, None),
        P("dom"),
        P("dom"),
        P("dom"),
        P("dom", None, None),
        P("dom", None),
    )
    return jax.shard_map(
        per_device,
        mesh=mesh,
        in_specs=placed,
        out_specs=(P("dom", None), P("dom", None), P()),
        check_vma=False,
    )
```

```python
import jax
import jax.numpy as jnp
from jax import lax
from jax.experimental import pallas as pl
from jax.experimental.pallas import tpu as pltpu
from jax.sharding import PartitionSpec as P

MESH = pl.DeviceIdType.MESH
N = 128
CHIPS = 64
F = 512
HALF = 256
R = 2048
TILE = 128
SLOTS = 8
HUBS = 4
TILES = 96
NEAR = 64
F32 = jnp.float32
BF16 = jnp.bfloat16
LIMIT = 62 * 1024 * 1024
STEP = 4
PAIR, HUB, HALO, TERM, BACK, HUB_BACK, SHARE, PAIR_BACK = range(8)


def whole_wait(ref, sem):
    pltpu.make_async_copy(ref, ref, sem).wait()


def one_hot(index, lanes):
    return (index == lanes).astype(F32).astype(BF16)


def transposed_dot(a, b):
    return lax.dot_general(a, b, (((0,), (0,)), ((), ())), preferred_element_type=F32)


def body(
    tiles_id, links, hub_s, send_ref, count_ref, feat_hbm, weight_ref, cot_hbm, tiles_hbm,
    out_ref, gfeat_ref, gweight_ref,
    tiles, near, far, cot, sums, gagg, term, column, picks, hub_picks,
    hub_slot, hub_chip, hub_in, halo_out, halo_in,
    term_out, term_in, share, gathered, back_out, back_in,
    hub_out, hub_back, hub_pair, hub_rows,
    load, send, recv,
):
    me = lax.axis_index("dom")
    chip, core = me // 2, lax.rem(me, 2)
    sibling = me + 1 - 2 * core

    loads = (
        pltpu.make_async_copy(feat_hbm, near.at[pl.ds(0, 16)], load.at[0]),
        pltpu.make_async_copy(tiles_hbm, tiles, load.at[1]),
        pltpu.make_async_copy(cot_hbm, cot, load.at[2]),
    )
    for copy in loads:
        copy.start()

    barrier = pltpu.get_barrier_semaphore()

    @pl.loop(1, N)
    def _(i):
        pl.semaphore_signal(
            barrier, inc=1, device_id=(lax.rem(me + i, N),), device_id_type=MESH
        )

    def remote(src, dst, slot, peer):
        return pltpu.make_async_remote_copy(
            src_ref=src, dst_ref=dst, send_sem=send.at[slot], recv_sem=recv.at[slot],
            device_id=(peer,), device_id_type=MESH,
        )

    slot_iota = lax.broadcasted_iota(jnp.int32, (SLOTS, N), 0)
    index = jnp.where(slot_iota < count_ref[...], send_ref[...], -1).astype(F32)
    index = jnp.concatenate([index, jnp.zeros((N - SLOTS, N), F32)], axis=0).T
    sub = lax.broadcasted_iota(jnp.int32, (TILE, TILE), 0)
    lane = lax.broadcasted_iota(jnp.int32, (TILE, TILE), 1)
    diagonal = lane == lax.rem(sub, SLOTS)
    for b in range(8):
        spread = jnp.broadcast_to(index[16 * b : 16 * b + 16, None, :], (16, SLOTS, N))
        chosen = jnp.where(diagonal, spread.reshape(TILE, TILE), 0.0)
        one = jnp.sum(chosen, axis=1, keepdims=True)
        column[pl.ds(b * TILE, TILE), :] = jnp.broadcast_to(one, (TILE, TILE)).astype(jnp.int32)

    hub_at = lax.broadcasted_iota(jnp.int32, (8, R), 0)
    hub_id = jnp.full((8, R), -1, jnp.int32)
    for j in range(HUBS):
        hub_id = jnp.where(hub_at == HUBS * core + j, hub_s[j], hub_id)
    sums[0] = jnp.zeros((TILE, F), F32)

    loads[0].wait()
    lanes = lax.broadcasted_iota(jnp.int32, (8, R), 1)
    hub_slot[0] = jnp.dot(
        one_hot(hub_id, lanes), near[pl.ds(0, 16)].reshape(R, F), preferred_element_type=F32
    ).astype(BF16)

    lanes = lax.broadcasted_iota(jnp.int32, (HALF, R), 1)
    for b in range(4):
        here = column[pl.ds(b * HALF, HALF), 0:1]
        rows = jnp.dot(
            one_hot(here, lanes), near[pl.ds(0, 16)].reshape(R, F), preferred_element_type=F32
        )
        halo_out[pl.ds(b * 32, 32)] = rows.reshape(32, SLOTS, F).astype(BF16)

    pl.semaphore_wait(barrier, N - 1)
    pair = remote(hub_slot.at[0], hub_slot.at[1], PAIR, sibling)
    pair.start()
    pltpu.make_async_copy(halo_out.at[me], halo_in.at[me], recv.at[HALO]).start()

    @pl.loop(1, 33)
    def _(i):
        peer = lax.rem(me + i, N)
        remote(halo_out.at[peer], halo_in.at[me], HALO, peer).start()

    pair.wait()
    hub_chip[0] = hub_slot[0] + hub_slot[1]
    pltpu.make_async_copy(hub_chip.at[0], hub_in.at[chip], recv.at[HUB]).start()

    @pl.loop(1, CHIPS)
    def _(i):
        peer = lax.rem(me + 2 * i, N)
        remote(hub_chip.at[0], hub_in.at[chip], HUB, peer).start()

    @pl.loop(33, N)
    def _(i):
        peer = lax.rem(me + i, N)
        remote(halo_out.at[peer], halo_in.at[me], HALO, peer).start()

    for b in range(8):
        picks_row = column[pl.ds(b * TILE, TILE), :].astype(F32).T.astype(jnp.int32)[0:1, :]

        @pl.loop(0, 16)
        def _(k):
            here = pl.ds(pl.multiple_of(k * TILE, TILE), TILE)
            picks[here, pl.ds(b * TILE, TILE)] = one_hot(picks_row, sub + k * TILE)

    hub_lane = lax.rem(lane, 8)
    hub_row = jnp.full((TILE, TILE), -1, jnp.int32)
    for j in range(HUBS):
        hub_row = jnp.where((hub_lane == HUBS * core + j) & (lane < 16), hub_s[j], hub_row)

    @pl.loop(0, 16)
    def _(k):
        here = pl.ds(pl.multiple_of(k * TILE, TILE), TILE)
        hub_picks[here, :] = one_hot(hub_row, sub + k * TILE)

    loads[1].wait()
    whole_wait(hub_in, recv.at[HUB])
    near[pl.ds(16, 4)] = hub_in[...].reshape(4, TILE, F)

    @pl.loop(0, NEAR // STEP)
    def _(g):
        for u in range(STEP):
            t = STEP * g + u
            sums[t + 1] = sums[links[0, t]] + jnp.dot(
                tiles[t], near[tiles_id[1, t]], preferred_element_type=F32
            )

    whole_wait(halo_in, recv.at[HALO])
    far[...] = halo_in[...].reshape(8, TILE, F)

    @pl.loop(0, (TILES - NEAR) // STEP)
    def _(g):
        for u in range(STEP):
            t = NEAR + STEP * g + u
            sums[t + 1] = sums[links[0, t]] + jnp.dot(
                tiles[t], far[jnp.maximum(tiles_id[1, t] - 20, 0)], preferred_element_type=F32
            )

    loads[2].wait()
    term[...] = jnp.zeros_like(term)
    weight = weight_ref[...]

    @pl.loop(0, 4)
    def _(k):
        parts = [sums[links[0, TILES + 4 * k + j]] for j in range(4)]
        agg = jnp.concatenate(parts, axis=0).astype(BF16)
        pre = jnp.dot(agg, weight, preferred_element_type=F32)
        sig = 0.5 * jnp.tanh(0.5 * pre) + 0.5
        here = pl.ds(pl.multiple_of(k * 512, 512), 512)
        out_ref[here, :] = (pre * sig).astype(BF16)
        gpre = (cot[here, :].astype(F32) * sig * (1.0 + pre * (1.0 - sig))).astype(BF16)
        term[...] += transposed_dot(agg, gpre)
        back = lax.dot_general(gpre, weight, (((1,), (1,)), ((), ())), preferred_element_type=F32)
        gagg[pl.ds(4 * k, 4)] = back.astype(BF16).reshape(4, TILE, F)

    whole = (term[...] * (1.0 / 512.0)).reshape(CHIPS, 8, F).astype(BF16)
    term_out[0] = whole[:, :, :HALF]
    term_out[1] = whole[:, :, HALF:]
    pltpu.make_async_copy(term_out.at[core, chip], term_in.at[me], recv.at[TERM]).start()

    @pl.loop(1, N)
    def _(i):
        peer = lax.rem(me + i, N)
        remote(term_out.at[lax.rem(peer, 2), peer // 2], term_in.at[me], TERM, peer).start()

    def spread_tile(t):
        sums[t + 1] = sums[links[1, t]] + transposed_dot(tiles[t], gagg[tiles_id[0, t]])

    @pl.loop(0, (TILES - NEAR) // STEP)
    def _(g):
        for u in range(STEP):
            spread_tile(NEAR + STEP * g + u)

    for b in range(8):
        rows = sums[links[1, TILES + 20 + b]]
        back_out[pl.ds(16 * b, 16)] = rows.reshape(16, SLOTS, F).astype(BF16)
    pltpu.make_async_copy(back_out.at[me], back_in.at[me], recv.at[BACK]).start()

    @pl.loop(1, N)
    def _(i):
        peer = lax.rem(me + i, N)
        remote(back_out.at[peer], back_in.at[me], BACK, peer).start()

    @pl.loop(0, NEAR // STEP)
    def _(g):
        for u in range(STEP):
            spread_tile(STEP * g + u)

    for b in range(4):
        rows = sums[links[1, TILES + 16 + b]].reshape(16, 8, F).astype(BF16)
        hub_out[0, pl.ds(16 * b, 16)] = rows[:, :, :HALF]
        hub_out[1, pl.ds(16 * b, 16)] = rows[:, :, HALF:]
    pltpu.make_async_copy(hub_out.at[core, chip], hub_back.at[me], recv.at[HUB_BACK]).start()

    @pl.loop(1, N)
    def _(i):
        peer = lax.rem(me + i, N)
        remote(hub_out.at[lax.rem(peer, 2), peer // 2], hub_back.at[me], HUB_BACK, peer).start()

    whole_wait(term_in, recv.at[TERM])
    share[0] = jnp.sum(term_in[...].astype(F32), axis=0).astype(BF16)
    pltpu.make_async_copy(share.at[0], gathered.at[core, chip], recv.at[SHARE]).start()

    @pl.loop(1, N)
    def _(i):
        peer = lax.rem(me + i, N)
        remote(share.at[0], gathered.at[core, chip], SHARE, peer).start()

    whole_wait(back_in, recv.at[BACK])

    @pl.loop(0, 8)
    def _(k):
        here = pl.ds(pl.multiple_of(k * HALF, HALF), HALF)
        back = jnp.dot(
            picks[here, :], back_in[...].reshape(N * SLOTS, F), preferred_element_type=F32
        )
        for j in range(2):
            at = links[1, TILES + 2 * k + j]
            sums[2 * k + j + 1 + 100] = sums[at] + back[j * TILE : j * TILE + TILE]

    whole_wait(hub_back, recv.at[HUB_BACK])
    hub_pair[0] = jnp.sum(hub_back[...].astype(F32), axis=0)
    pair = remote(hub_pair.at[0], hub_pair.at[1], PAIR_BACK, sibling)
    pair.start()
    pair.wait()
    hub_rows[...] = jnp.zeros_like(hub_rows)
    first = jnp.where(core == 0, hub_pair[0], hub_pair[1])
    second = jnp.where(core == 0, hub_pair[1], hub_pair[0])
    total = jnp.concatenate([first, second], axis=1)
    upper = total.astype(BF16).astype(F32)
    hub_rows[pl.ds(0, 16), :] = jnp.concatenate([upper, total - upper], axis=0).astype(BF16)

    @pl.loop(0, 8)
    def _(k):
        here = pl.ds(pl.multiple_of(k * HALF, HALF), HALF)
        hub = jnp.dot(hub_picks[here, :], hub_rows[...], preferred_element_type=F32)
        mine = sums[pl.ds(2 * k + 101, 2)].reshape(HALF, F)
        gfeat_ref[here, :] = (mine + hub).astype(BF16)

    whole_wait(gathered, recv.at[SHARE])
    for q in range(2):
        gweight_ref[:, :, q * HALF : q * HALF + HALF] = gathered[q].astype(F32)

    whole_wait(hub_in.at[pl.ds(0, CHIPS - 1)], send.at[HUB])
    whole_wait(halo_in.at[pl.ds(0, N - 1)], send.at[HALO])
    whole_wait(term_in.at[pl.ds(0, N - 1)], send.at[TERM])
    whole_wait(back_in.at[pl.ds(0, N - 1)], send.at[BACK])
    whole_wait(hub_back.at[pl.ds(0, N - 1)], send.at[HUB_BACK])
    whole_wait(term_in.at[pl.ds(0, N - 1)], send.at[SHARE])


def per_device(
    features, weight, cotangent, tile_values, tile_rows, tile_cols, hub_rows, send_rows, send_count
):
    ids = jnp.stack([tile_rows, tile_cols])
    blocks = jnp.broadcast_to(jnp.arange(32, dtype=jnp.int32), (2, 32))
    asked = jnp.concatenate([ids, blocks], axis=1)
    place = jnp.minimum(jnp.arange(128, dtype=jnp.int32), TILES)
    number = jnp.arange(TILES, dtype=jnp.int32)
    before = (ids[:, None, :] == asked[:, :, None]) & (number[None, :] < place[:, None])
    links = jnp.max(jnp.where(before, number + 1, 0), axis=2)

    smem = pl.BlockSpec(memory_space=pltpu.SMEM)
    vmem = pl.BlockSpec(memory_space=pltpu.VMEM)
    anywhere = pl.BlockSpec(memory_space=pl.ANY)
    output, grad_features, grad_weight = pl.pallas_call(
        body,
        out_shape=(
            jax.ShapeDtypeStruct((R, F), BF16),
            jax.ShapeDtypeStruct((R, F), BF16),
            jax.ShapeDtypeStruct((CHIPS, 8, F), F32),
        ),
        in_specs=[smem] * 3 + [vmem] * 2 + [anywhere, vmem, anywhere, anywhere],
        out_specs=(vmem, vmem, vmem),
        scratch_shapes=[
            pltpu.VMEM((TILES, TILE, TILE), BF16),
            pltpu.VMEM((20, TILE, F), BF16),
            pltpu.VMEM((8, TILE, F), BF16),
            pltpu.VMEM((R, F), BF16),
            pltpu.VMEM((TILES + 21, TILE, F), F32),
            pltpu.VMEM((16, TILE, F), BF16),
            pltpu.VMEM((F, F), F32),
            pltpu.VMEM((N * SLOTS, TILE), jnp.int32),
            pltpu.VMEM((R, N * SLOTS), BF16),
            pltpu.VMEM((R, TILE), BF16),
            pltpu.VMEM((2, 8, F), BF16),
            pltpu.VMEM((1, 8, F), BF16),
            pltpu.VMEM((CHIPS, 8, F), BF16),
            pltpu.VMEM((N, SLOTS, F), BF16),
            pltpu.VMEM((N, SLOTS, F), BF16),
            pltpu.VMEM((2, CHIPS, 8, HALF), BF16),
            pltpu.VMEM((N, 8, HALF), BF16),
            pltpu.VMEM((1, 8, HALF), BF16),
            pltpu.VMEM((2, CHIPS, 8, HALF), BF16),
            pltpu.VMEM((N, SLOTS, F), BF16),
            pltpu.VMEM((N, SLOTS, F), BF16),
            pltpu.VMEM((2, CHIPS, 8, HALF), BF16),
            pltpu.VMEM((N, 8, HALF), BF16),
            pltpu.VMEM((2, 8, HALF), F32),
            pltpu.VMEM((TILE, F), BF16),
            pltpu.SemaphoreType.DMA((3,)),
            pltpu.SemaphoreType.DMA((8,)),
            pltpu.SemaphoreType.DMA((8,)),
        ],
        compiler_params=pltpu.CompilerParams(
            collective_id=0, has_side_effects=True, vmem_limit_bytes=LIMIT
        ),
        name="graph_layer",
    )(
        ids, links, hub_rows, send_rows[0].T, send_count, features.reshape(16, TILE, F), weight,
        cotangent, tile_values,
    )
    return output, grad_features, grad_weight.reshape(F, F)


def solution(mesh):
    placed = (
        P("dom", None),
        P(),
        P("dom", None),
        P("dom", None, None),
        P("dom"),
        P("dom"),
        P("dom"),
        P("dom", None, None),
        P("dom", None),
    )
    return jax.shard_map(
        per_device,
        mesh=mesh,
        in_specs=placed,
        out_specs=(P("dom", None), P("dom", None), P()),
        check_vma=False,
    )
```

```python
import jax
import jax.numpy as jnp
from jax import lax
from jax.experimental import pallas as pl
from jax.experimental.pallas import tpu as pltpu
from jax.sharding import PartitionSpec as P

MESH = pl.DeviceIdType.MESH
N = 128
CHIPS = 64
F = 512
HALF = 256
R = 2048
TILE = 128
SLOTS = 8
HUBS = 4
TILES = 96
NEAR = 64
F32 = jnp.float32
BF16 = jnp.bfloat16
LIMIT = 62 * 1024 * 1024
STEP = 4
(
    PAIR, HUB, HUB_SHARE, HALO, TERM_PAIR, TERM, BACK, BACK_PAIR, HUB_BACK, SHARE, SHARE_PAIR,
    LAST_PAIR,
) = range(12)
MORE = TILES + 1


def whole_wait(ref, sem):
    pltpu.make_async_copy(ref, ref, sem).wait()


def one_hot(index, lanes):
    return (index == lanes).astype(F32).astype(BF16)


def transposed_dot(a, b):
    return lax.dot_general(a, b, (((0,), (0,)), ((), ())), preferred_element_type=F32)


def body(
    rows_s, cols_s, hub_s, rows_ref, cols_ref, send_ref, count_ref, feat_hbm, weight_ref, cot_hbm,
    tiles_hbm,
    out_hbm, gfeat_hbm, gweight_hbm,
    tiles, near, far, cot, out, sums, gagg, term, turned, column, picks, hub_picks, ids, links_v,
    hub_own, hub_got, hub_half, hub_in, halo_out, halo_in,
    term_out, term_got, term_half, term_in, share, gathered, back_out, back_in,
    hub_out, hub_back_got, hub_back_half, hub_back, hub_pair, hub_rows,
    links, load, store, send, recv,
):
    me = lax.axis_index("dom")
    chip, core = me // 2, lax.rem(me, 2)
    sibling = me + 1 - 2 * core
    other = 1 - core

    loads = (
        pltpu.make_async_copy(feat_hbm, near.at[pl.ds(0, 16)], load.at[0]),
        pltpu.make_async_copy(tiles_hbm, tiles, load.at[1]),
        pltpu.make_async_copy(cot_hbm, cot, load.at[2]),
    )
    for copy in loads:
        copy.start()

    barrier = pltpu.get_barrier_semaphore()

    @pl.loop(1, N)
    def _(i):
        pl.semaphore_signal(
            barrier, inc=1, device_id=(lax.rem(me + i, N),), device_id_type=MESH
        )

    def remote(src, dst, slot, peer):
        return pltpu.make_async_remote_copy(
            src_ref=src, dst_ref=dst, send_sem=send.at[slot], recv_sem=recv.at[slot],
            device_id=(peer,), device_id_type=MESH,
        )

    def link(q, t):
        return jnp.clip(links[q, t], 0, TILES)

    def to_plane(source, target, slot):
        @pl.loop(1, CHIPS)
        def _(j):
            there = lax.rem(chip + 23 * j, CHIPS)
            remote(source(there), target, slot, 2 * there + core).start()

    slot_iota = lax.broadcasted_iota(jnp.int32, (SLOTS, N), 0)
    index = jnp.where(slot_iota < count_ref[...], send_ref[...], -1).astype(F32)
    turned[...] = jnp.concatenate([index, jnp.zeros((N - SLOTS, N), F32)], axis=0).T
    sub = lax.broadcasted_iota(jnp.int32, (TILE, TILE), 0)
    lane = lax.broadcasted_iota(jnp.int32, (TILE, TILE), 1)
    diagonal = lax.broadcasted_iota(jnp.int32, (HALF, TILE), 1) == lax.rem(
        lax.broadcasted_iota(jnp.int32, (HALF, TILE), 0), SLOTS
    )
    for b in range(4):
        part = turned[pl.ds(b, 32, stride=4), :]
        spread = jnp.broadcast_to(part[:, None, :], (32, SLOTS, N)).reshape(HALF, TILE)
        one = jnp.sum(jnp.where(diagonal, spread, 0.0), axis=1, keepdims=True)
        column[pl.ds(b * HALF, HALF), :] = jnp.broadcast_to(one, (HALF, TILE)).astype(jnp.int32)

    hub_at = lax.broadcasted_iota(jnp.int32, (8, R), 0)
    hub_id = jnp.full((8, R), -1, jnp.int32)
    for j in range(HUBS):
        hub_id = jnp.where(hub_at == HUBS * core + j, hub_s[j], hub_id)

    loads[0].wait()
    lanes = lax.broadcasted_iota(jnp.int32, (8, R), 1)
    rows = jnp.dot(
        one_hot(hub_id, lanes), near[pl.ds(0, 16)].reshape(R, F), preferred_element_type=F32
    ).astype(BF16)
    hub_own[0] = rows[:, :HALF]
    hub_own[1] = rows[:, HALF:]

    def gather(block):
        here = column[pl.ds(pl.multiple_of(block * HALF, HALF), HALF), 0:1]
        rows = jnp.dot(
            one_hot(here, lax.broadcasted_iota(jnp.int32, (HALF, R), 1)),
            near[pl.ds(0, 16)].reshape(R, F), preferred_element_type=F32,
        )
        halo_out[block] = rows.reshape(32, SLOTS, F).astype(BF16)

    def send_block(block, first):
        @pl.loop(first, 32)
        def _(j):
            there = lax.rem(me // 4 + 11 * j, 32)
            remote(
                halo_out.at[block, there], halo_in.at[me], HALO, 4 * there + block
            ).start()

    quarter = lax.rem(me, 4)
    gather(quarter)
    pl.semaphore_wait(barrier, N - 1)
    pair = remote(hub_own.at[other], hub_got.at[0], PAIR, sibling)
    pair.start()
    pltpu.make_async_copy(halo_out.at[quarter, me // 4], halo_in.at[me], recv.at[HALO]).start()
    send_block(quarter, 1)
    gather(lax.rem(quarter + 1, 4))
    pair.wait()
    hub_half[0] = hub_own[core] + hub_got[0]
    pltpu.make_async_copy(hub_half.at[0], hub_in.at[core, chip], recv.at[HUB]).start()
    to_plane(lambda there: hub_half.at[0], hub_in.at[core, chip], HUB)
    send_block(lax.rem(quarter + 1, 4), 0)
    for b in range(2, 4):
        gather(lax.rem(quarter + b, 4))
        send_block(lax.rem(quarter + b, 4), 0)

    ids[...] = jnp.zeros_like(ids)
    ids[0:1, 0:TILES] = rows_ref[...]
    ids[1:2, 0:TILES] = cols_ref[...]
    links_v[...] = jnp.zeros_like(links_v)
    for q in range(2):
        keys = jnp.broadcast_to(ids[q : q + 1, :], (TILE, TILE))
        asked = jnp.where(lane < TILES, keys, lane - TILES)
        before = (keys.T == asked) & (sub < jnp.minimum(lane, TILES))
        number = jnp.where(before, sub + 1, 0)
        links_v[q : q + 1, :] = jnp.max(number, axis=0, keepdims=True)
    copy_links = pltpu.make_async_copy(links_v, links, load.at[3])
    copy_links.start()
    sums[0] = jnp.zeros((TILE, F), F32)

    for b in range(8):
        picks_row = column[pl.ds(b * TILE, TILE), :].astype(F32).T.astype(jnp.int32)[0:1, :]

        @pl.loop(0, 16)
        def _(k):
            here = pl.ds(pl.multiple_of(k * TILE, TILE), TILE)
            picks[here, pl.ds(b * TILE, TILE)] = one_hot(picks_row, sub + k * TILE)

    hub_lane = lax.rem(lane, 8)
    hub_row = jnp.full((TILE, TILE), -1, jnp.int32)
    for j in range(HUBS):
        hub_row = jnp.where((hub_lane == HUBS * core + j) & (lane < 16), hub_s[j], hub_row)

    @pl.loop(0, 16)
    def _(k):
        here = pl.ds(pl.multiple_of(k * TILE, TILE), TILE)
        hub_picks[here, :] = one_hot(hub_row, sub + k * TILE)

    whole_wait(hub_in.at[core], recv.at[HUB])
    pair = remote(hub_in.at[core], hub_in.at[core], HUB_SHARE, sibling)
    pair.start()
    loads[1].wait()
    copy_links.wait()
    pair.wait()
    for b in range(4):
        for q in range(2):
            near[16 + b, :, q * HALF : q * HALF + HALF] = hub_in[q, pl.ds(16 * b, 16)].reshape(
                TILE, HALF
            )

    @pl.loop(0, NEAR // STEP)
    def _(g):
        for u in range(STEP):
            t = STEP * g + u
            sums[t + 1] = sums[link(0, t)] + jnp.dot(
                tiles[t], near[cols_s[t]], preferred_element_type=F32
            )

    whole_wait(halo_in, recv.at[HALO])
    far[...] = halo_in[...].reshape(8, TILE, F)

    @pl.loop(0, (TILES - NEAR) // STEP)
    def _(g):
        for u in range(STEP):
            t = NEAR + STEP * g + u
            sums[t + 1] = sums[link(0, t)] + jnp.dot(
                tiles[t], far[jnp.maximum(cols_s[t] - 20, 0)], preferred_element_type=F32
            )

    loads[2].wait()
    term[...] = jnp.zeros_like(term)
    weight = weight_ref[...]

    @pl.loop(0, 4)
    def _(k):
        parts = [sums[link(0, TILES + 4 * k + j)] for j in range(4)]
        agg = jnp.concatenate(parts, axis=0).astype(BF16)
        pre = jnp.dot(agg, weight, preferred_element_type=F32)
        sig = 0.5 * jnp.tanh(0.5 * pre) + 0.5
        here = pl.ds(pl.multiple_of(k * 512, 512), 512)
        out[here, :] = (pre * sig).astype(BF16)
        gpre = (cot[here, :].astype(F32) * sig * (1.0 + pre * (1.0 - sig))).astype(BF16)
        term[...] += transposed_dot(agg, gpre)
        back = lax.dot_general(gpre, weight, (((1,), (1,)), ((), ())), preferred_element_type=F32)
        gagg[pl.ds(4 * k, 4)] = back.astype(BF16).reshape(4, TILE, F)

    save_out = pltpu.make_async_copy(out, out_hbm, store.at[0])
    save_out.start()
    whole = (term[...] * (1.0 / 512.0)).reshape(CHIPS, 8, F).astype(BF16)
    term_out[0] = whole[:, :, :HALF]
    term_out[1] = whole[:, :, HALF:]
    pair = remote(term_out.at[other], term_got, TERM_PAIR, sibling)
    pair.start()

    def spread_tile(t):
        sums[t + 1] = sums[link(1, t)] + transposed_dot(tiles[t], gagg[rows_s[t]])

    @pl.loop(0, 16 // STEP)
    def _(g):
        for u in range(STEP):
            spread_tile(NEAR + STEP * g + u)

    pair.wait()
    term_half[...] = (term_out[core].astype(F32) + term_got[...].astype(F32)).astype(BF16)
    pltpu.make_async_copy(term_half.at[chip], term_in.at[chip], recv.at[TERM]).start()
    to_plane(lambda there: term_half.at[there], term_in.at[chip], TERM)

    @pl.loop(16 // STEP, (TILES - NEAR) // STEP)
    def _(g):
        for u in range(STEP):
            spread_tile(NEAR + STEP * g + u)

    for b in range(8):
        rows = sums[link(1, TILES + 20 + b)]
        back_out[pl.ds(16 * b, 16)] = rows.reshape(16, SLOTS, F).astype(BF16)
    landing = back_in.at[quarter, me // 4]
    pltpu.make_async_copy(back_out.at[me], landing, recv.at[BACK]).start()

    @pl.loop(1, N)
    def _(i):
        peer = lax.rem(me + 37 * i, N)
        remote(back_out.at[peer], landing, BACK, peer).start()

    @pl.loop(0, NEAR // STEP)
    def _(g):
        for u in range(STEP):
            spread_tile(STEP * g + u)

    for b in range(4):
        rows = sums[link(1, TILES + 16 + b)].reshape(16, 8, F).astype(BF16)
        hub_out[0, pl.ds(16 * b, 16)] = rows[:, :, :HALF]
        hub_out[1, pl.ds(16 * b, 16)] = rows[:, :, HALF:]
    pair = remote(hub_out.at[other], hub_back_got, BACK_PAIR, sibling)
    pair.start()

    whole_wait(term_in, recv.at[TERM])
    share[0] = jnp.sum(term_in[...].astype(F32), axis=0).astype(BF16)
    pltpu.make_async_copy(share.at[0], gathered.at[core, chip], recv.at[SHARE]).start()
    to_plane(lambda there: share.at[0], gathered.at[core, chip], SHARE)

    pair.wait()
    hub_back_half[...] = (
        hub_out[core].astype(F32) + hub_back_got[...].astype(F32)
    ).astype(BF16)
    pltpu.make_async_copy(hub_back_half.at[chip], hub_back.at[chip], recv.at[HUB_BACK]).start()
    to_plane(lambda there: hub_back_half.at[there], hub_back.at[chip], HUB_BACK)

    whole_wait(back_in, recv.at[BACK])

    @pl.loop(0, 8)
    def _(k):
        here = pl.ds(pl.multiple_of(k * HALF, HALF), HALF)
        back = jnp.dot(
            picks[here, :], back_in[...].reshape(N * SLOTS, F), preferred_element_type=F32
        )
        for j in range(2):
            at = link(1, TILES + 2 * k + j)
            sums[2 * k + j + MORE] = sums[at] + back[j * TILE : j * TILE + TILE]

    whole_wait(gathered.at[core], recv.at[SHARE])
    share_pair = remote(gathered.at[core], gathered.at[core], SHARE_PAIR, sibling)
    share_pair.start()

    whole_wait(hub_back, recv.at[HUB_BACK])
    hub_pair[0] = jnp.sum(hub_back[...].astype(F32), axis=0)
    pair = remote(hub_pair.at[0], hub_pair.at[1], LAST_PAIR, sibling)
    pair.start()
    save_out.wait()
    share_pair.wait()
    save_weight = pltpu.make_async_copy(gathered, gweight_hbm, store.at[1])
    save_weight.start()
    pair.wait()
    hub_rows[...] = jnp.zeros_like(hub_rows)
    first = jnp.where(core == 0, hub_pair[0], hub_pair[1])
    second = jnp.where(core == 0, hub_pair[1], hub_pair[0])
    total = jnp.concatenate([first, second], axis=1)
    upper = total.astype(BF16).astype(F32)
    hub_rows[pl.ds(0, 16), :] = jnp.concatenate([upper, total - upper], axis=0).astype(BF16)

    @pl.loop(0, 8)
    def _(k):
        here = pl.ds(pl.multiple_of(k * HALF, HALF), HALF)
        hub = jnp.dot(hub_picks[here, :], hub_rows[...], preferred_element_type=F32)
        mine = sums[pl.ds(2 * k + MORE, 2)].reshape(HALF, F)
        out[here, :] = (mine + hub).astype(BF16)

    save_grad = pltpu.make_async_copy(out, gfeat_hbm, store.at[0])
    save_grad.start()
    whole_wait(hub_back.at[pl.ds(0, CHIPS - 1)], send.at[HUB])
    whole_wait(halo_in.at[pl.ds(0, N - 1)], send.at[HALO])
    whole_wait(hub_back.at[pl.ds(0, CHIPS - 1)], send.at[TERM])
    whole_wait(halo_in.at[pl.ds(0, N - 1)], send.at[BACK])
    whole_wait(hub_back.at[pl.ds(0, CHIPS - 1)], send.at[HUB_BACK])
    whole_wait(hub_back.at[pl.ds(0, CHIPS - 1)], send.at[SHARE])
    save_grad.wait()
    save_weight.wait()


def finish(out_in, gfeat_in, gathered_ref, out_ref, gfeat_ref, gweight_ref, sems):
    copies = []
    for a, (src, dst) in enumerate(((out_in, out_ref), (gfeat_in, gfeat_ref))):
        for b in range(4):
            here = pl.ds(b * 512, 512)
            copies.append(pltpu.make_async_copy(src.at[here], dst.at[here], sems.at[4 * a + b]))
    for copy in copies:
        copy.start()
    for q in range(2):
        gweight_ref[:, :, q * HALF : q * HALF + HALF] = gathered_ref[q].astype(F32)
    for copy in copies:
        copy.wait()


def per_device(
    features, weight, cotangent, tile_values, tile_rows, tile_cols, hub_rows, send_rows, send_count
):
    smem = pl.BlockSpec(memory_space=pltpu.SMEM)
    vmem = pl.BlockSpec(memory_space=pltpu.VMEM)
    anywhere = pl.BlockSpec(memory_space=pl.ANY)
    plane = (2, CHIPS, 8, HALF)
    output, grad_features, gathered = pl.pallas_call(
        body,
        out_shape=(
            jax.ShapeDtypeStruct((R, F), BF16),
            jax.ShapeDtypeStruct((R, F), BF16),
            jax.ShapeDtypeStruct(plane, BF16),
        ),
        in_specs=[smem] * 3 + [vmem] * 4 + [anywhere, vmem, anywhere, anywhere],
        out_specs=(anywhere,) * 3,
        scratch_shapes=[
            pltpu.VMEM((TILES, TILE, TILE), BF16),
            pltpu.VMEM((20, TILE, F), BF16),
            pltpu.VMEM((8, TILE, F), BF16),
            pltpu.VMEM((R, F), BF16),
            pltpu.VMEM((R, F), BF16),
            pltpu.VMEM((MORE + 16, TILE, F), F32),
            pltpu.VMEM((16, TILE, F), BF16),
            pltpu.VMEM((F, F), F32),
            pltpu.VMEM((TILE, TILE), F32),
            pltpu.VMEM((N * SLOTS, TILE), jnp.int32),
            pltpu.VMEM((R, N * SLOTS), BF16),
            pltpu.VMEM((R, TILE), BF16),
            pltpu.VMEM((8, TILE), jnp.int32),
            pltpu.VMEM((8, TILE), jnp.int32),
            pltpu.VMEM((2, 8, HALF), BF16),
            pltpu.VMEM((1, 8, HALF), BF16),
            pltpu.VMEM((1, 8, HALF), BF16),
            pltpu.VMEM(plane, BF16),
            pltpu.VMEM((4, 32, SLOTS, F), BF16),
            pltpu.VMEM((N, SLOTS, F), BF16),
            pltpu.VMEM(plane, BF16),
            pltpu.VMEM(plane[1:], BF16),
            pltpu.VMEM(plane[1:], BF16),
            pltpu.VMEM(plane[1:], BF16),
            pltpu.VMEM((1, 8, HALF), BF16),
            pltpu.VMEM(plane, BF16),
            pltpu.VMEM((N, SLOTS, F), BF16),
            pltpu.VMEM((4, 32, SLOTS, F), BF16),
            pltpu.VMEM(plane, BF16),
            pltpu.VMEM(plane[1:], BF16),
            pltpu.VMEM(plane[1:], BF16),
            pltpu.VMEM(plane[1:], BF16),
            pltpu.VMEM((2, 8, HALF), F32),
            pltpu.VMEM((TILE, F), BF16),
            pltpu.SMEM((8, TILE), jnp.int32),
            pltpu.SemaphoreType.DMA((4,)),
            pltpu.SemaphoreType.DMA((2,)),
            pltpu.SemaphoreType.DMA((12,)),
            pltpu.SemaphoreType.DMA((12,)),
        ],
        compiler_params=pltpu.CompilerParams(
            collective_id=0, has_side_effects=True, vmem_limit_bytes=LIMIT
        ),
        name="graph_layer",
    )(
        tile_rows, tile_cols, hub_rows, tile_rows.reshape(1, TILES), tile_cols.reshape(1, TILES),
        send_rows[0].T, send_count, features.reshape(16, TILE, F), weight, cotangent, tile_values,
    )
    output, grad_features, grad_weight = pl.pallas_call(
        finish,
        out_shape=(
            jax.ShapeDtypeStruct((R, F), BF16),
            jax.ShapeDtypeStruct((R, F), BF16),
            jax.ShapeDtypeStruct((CHIPS, 8, F), F32),
        ),
        in_specs=[anywhere, anywhere, vmem],
        out_specs=(anywhere, anywhere, vmem),
        scratch_shapes=[pltpu.SemaphoreType.DMA((8,))],
        name="finish",
    )(output, grad_features, gathered)
    return output, grad_features, grad_weight.reshape(F, F)


def solution(mesh):
    placed = (
        P("dom", None),
        P(),
        P("dom", None),
        P("dom", None, None),
        P("dom"),
        P("dom"),
        P("dom"),
        P("dom", None, None),
        P("dom", None),
    )
    return jax.shard_map(
        per_device,
        mesh=mesh,
        in_specs=placed,
        out_specs=(P("dom", None), P("dom", None), P()),
        check_vma=False,
    )
```

```python
import jax
import jax.numpy as jnp
from jax import lax
from jax.experimental import pallas as pl
from jax.experimental.pallas import tpu as pltpu
from jax.sharding import PartitionSpec as P

MESH = pl.DeviceIdType.MESH
N = 128
CHIPS = 64
F = 512
HALF = 256
R = 2048
TILE = 128
SLOTS = 8
HUBS = 4
TILES = 96
NEAR = 64
F32 = jnp.float32
BF16 = jnp.bfloat16
LIMIT = 62 * 1024 * 1024
STEP = 8
(
    PAIR, HUB, HUB_SHARE, HALO, TERM_PAIR, TERM, BACK, BACK_PAIR, HUB_BACK, SHARE, SHARE_PAIR,
    LAST_PAIR,
) = range(12)
MORE = TILES + 1


def whole_wait(ref, sem):
    pltpu.make_async_copy(ref, ref, sem).wait()


def one_hot(index, lanes):
    return (index == lanes).astype(F32).astype(BF16)


def transposed_dot(a, b):
    return lax.dot_general(a, b, (((0,), (0,)), ((), ())), preferred_element_type=F32)


def body(
    rows_s, cols_s, hub_s, rows_ref, cols_ref, send_ref, count_ref, feat_hbm, weight_ref, cot_hbm,
    tiles_hbm,
    out_hbm, gfeat_hbm, gweight_hbm,
    tiles, near, far, cot, out, sums, gagg, term, turned, column, picks, hub_picks, ids, links_v,
    hub_own, hub_got, hub_half, hub_in, halo_out, halo_in,
    term_out, term_got, term_half, term_in, share, gathered, back_out, back_in,
    hub_back_got, hub_back_half, hub_back, hub_pair, hub_rows,
    links, load, store, send, recv,
):
    me = lax.axis_index("dom")
    chip, core = me // 2, lax.rem(me, 2)
    sibling = me + 1 - 2 * core
    other = 1 - core

    loads = (
        pltpu.make_async_copy(feat_hbm, near.at[pl.ds(0, 16)], load.at[0]),
        pltpu.make_async_copy(tiles_hbm, tiles, load.at[1]),
        pltpu.make_async_copy(cot_hbm, cot, load.at[2]),
    )
    for copy in loads:
        copy.start()

    barrier = pltpu.get_barrier_semaphore()

    @pl.loop(1, N)
    def _(i):
        pl.semaphore_signal(
            barrier, inc=1, device_id=(lax.rem(me + i, N),), device_id_type=MESH
        )

    def remote(src, dst, slot, peer):
        return pltpu.make_async_remote_copy(
            src_ref=src, dst_ref=dst, send_sem=send.at[slot], recv_sem=recv.at[slot],
            device_id=(peer,), device_id_type=MESH,
        )

    def link(q, t):
        return jnp.clip(links[q, t], 0, TILES)

    at_x, at_z, at_y = chip // 16, lax.rem(chip // 4, 4), lax.rem(chip, 4)

    def moved(dx, dz, dy):
        return (
            lax.rem(at_x + dx, 4) * 16 + lax.rem(at_z + dz, 4) * 4 + lax.rem(at_y + dy, 4)
        )

    def to_plane(source, target, slot):
        @pl.loop(1, CHIPS)
        def _(j):
            step = lax.rem(j * 43, CHIPS)
            there = moved(step // 16, lax.rem(step // 4, 4), lax.rem(step, 4))
            remote(source(there), target, slot, 2 * there + core).start()

    slot_iota = lax.broadcasted_iota(jnp.int32, (SLOTS, N), 0)
    index = jnp.where(slot_iota < count_ref[...], send_ref[...], -1).astype(F32)
    turned[...] = jnp.concatenate([index, jnp.zeros((N - SLOTS, N), F32)], axis=0).T
    sub = lax.broadcasted_iota(jnp.int32, (TILE, TILE), 0)
    lane = lax.broadcasted_iota(jnp.int32, (TILE, TILE), 1)
    diagonal = lax.broadcasted_iota(jnp.int32, (HALF, TILE), 1) == lax.rem(
        lax.broadcasted_iota(jnp.int32, (HALF, TILE), 0), SLOTS
    )
    for b in range(4):
        part = turned[pl.ds(b, 32, stride=4), :]
        spread = jnp.broadcast_to(part[:, None, :], (32, SLOTS, N)).reshape(HALF, TILE)
        one = jnp.sum(jnp.where(diagonal, spread, 0.0), axis=1, keepdims=True)
        column[pl.ds(b * HALF, HALF), :] = jnp.broadcast_to(one, (HALF, TILE)).astype(jnp.int32)

    hub_at = lax.broadcasted_iota(jnp.int32, (8, R), 0)
    hub_id = jnp.full((8, R), -1, jnp.int32)
    for j in range(HUBS):
        hub_id = jnp.where(hub_at == HUBS * core + j, hub_s[j], hub_id)

    loads[0].wait()
    lanes = lax.broadcasted_iota(jnp.int32, (8, R), 1)
    rows = jnp.dot(
        one_hot(hub_id, lanes), near[pl.ds(0, 16)].reshape(R, F), preferred_element_type=F32
    ).astype(BF16)
    hub_own[0] = rows[:, :HALF]
    hub_own[1] = rows[:, HALF:]

    def gather(block):
        here = column[pl.ds(pl.multiple_of(block * HALF, HALF), HALF), 0:1]
        rows = jnp.dot(
            one_hot(here, lax.broadcasted_iota(jnp.int32, (HALF, R), 1)),
            near[pl.ds(0, 16)].reshape(R, F), preferred_element_type=F32,
        )
        halo_out[block] = rows.reshape(32, SLOTS, F).astype(BF16)

    quarter = lax.rem(me, 4)

    def block_of(b):
        return 2 * lax.rem(at_y + b // 2, 2) + lax.rem(core + b, 2)

    def send_block(b):
        block = block_of(b)

        @pl.loop(1 if b == 0 else 0, 32)
        def _(j):
            step = lax.rem(j * 11, 32)
            there = moved(step // 8, lax.rem(step // 2, 4), 2 * lax.rem(step, 2) + b // 2)
            peer = 2 * there + lax.rem(block, 2)
            remote(halo_out.at[block, peer // 4], halo_in.at[me], HALO, peer).start()

    gather(quarter)
    pl.semaphore_wait(barrier, N - 1)
    pair = remote(hub_own.at[other], hub_got.at[0], PAIR, sibling)
    pair.start()
    pltpu.make_async_copy(halo_out.at[quarter, me // 4], halo_in.at[me], recv.at[HALO]).start()
    send_block(0)
    gather(block_of(1))
    pair.wait()
    hub_half[0] = hub_own[core] + hub_got[0]
    pltpu.make_async_copy(hub_half.at[0], hub_in.at[core, chip], recv.at[HUB]).start()
    to_plane(lambda there: hub_half.at[0], hub_in.at[core, chip], HUB)
    send_block(1)
    for b in range(2, 4):
        gather(block_of(b))
        send_block(b)

    ids[...] = jnp.zeros_like(ids)
    ids[0:1, 0:TILES] = rows_ref[...]
    ids[1:2, 0:TILES] = cols_ref[...]
    links_v[...] = jnp.zeros_like(links_v)
    for q in range(2):
        keys = jnp.broadcast_to(ids[q : q + 1, :], (TILE, TILE))
        asked = jnp.where(lane < TILES, keys, lane - TILES)
        before = (keys.T == asked) & (sub < jnp.minimum(lane, TILES))
        number = jnp.where(before, sub + 1, 0)
        links_v[q : q + 1, :] = jnp.max(number, axis=0, keepdims=True)
    copy_links = pltpu.make_async_copy(links_v, links, load.at[3])
    copy_links.start()
    sums[0] = jnp.zeros((TILE, F), F32)

    for b in range(8):
        picks_row = column[pl.ds(b * TILE, TILE), :].astype(F32).T.astype(jnp.int32)[0:1, :]

        @pl.loop(0, 16)
        def _(k):
            here = pl.ds(pl.multiple_of(k * TILE, TILE), TILE)
            picks[here, pl.ds(b * TILE, TILE)] = one_hot(picks_row, sub + k * TILE)

    hub_lane = lax.rem(lane, 8)
    hub_row = jnp.full((TILE, TILE), -1, jnp.int32)
    for j in range(HUBS):
        hub_row = jnp.where((hub_lane == HUBS * core + j) & (lane < 16), hub_s[j], hub_row)

    @pl.loop(0, 16)
    def _(k):
        here = pl.ds(pl.multiple_of(k * TILE, TILE), TILE)
        hub_picks[here, :] = one_hot(hub_row, sub + k * TILE)

    whole_wait(hub_in.at[core], recv.at[HUB])
    pair = remote(hub_in.at[core], hub_in.at[core], HUB_SHARE, sibling)
    pair.start()
    loads[1].wait()
    copy_links.wait()
    pair.wait()
    for b in range(4):
        for q in range(2):
            near[16 + b, :, q * HALF : q * HALF + HALF] = hub_in[q, pl.ds(16 * b, 16)].reshape(
                TILE, HALF
            )

    @pl.loop(0, NEAR // STEP)
    def _(g):
        for u in range(STEP):
            t = STEP * g + u
            sums[t + 1] = sums[link(0, t)] + jnp.dot(
                tiles[t], near[cols_s[t]], preferred_element_type=F32
            )

    whole_wait(halo_in, recv.at[HALO])
    far[...] = halo_in[...].reshape(8, TILE, F)

    @pl.loop(0, (TILES - NEAR) // STEP)
    def _(g):
        for u in range(STEP):
            t = NEAR + STEP * g + u
            sums[t + 1] = sums[link(0, t)] + jnp.dot(
                tiles[t], far[jnp.maximum(cols_s[t] - 20, 0)], preferred_element_type=F32
            )

    loads[2].wait()
    weight = weight_ref[...]

    agg = jnp.concatenate([sums[link(0, TILES + j)] for j in range(16)], axis=0).astype(BF16)
    near[pl.ds(0, 16)] = agg.reshape(16, TILE, F)
    pre = jnp.dot(agg, weight, preferred_element_type=F32)
    sig = 0.5 * jnp.tanh(0.5 * pre) + 0.5
    out[...] = (pre * sig).astype(BF16)
    gpre = (cot[...].astype(F32) * sig * (1.0 + pre * (1.0 - sig))).astype(BF16)
    cot[...] = gpre
    back = lax.dot_general(gpre, weight, (((1,), (1,)), ((), ())), preferred_element_type=F32)
    gagg[...] = back.astype(BF16).reshape(16, TILE, F)

    save_out = pltpu.make_async_copy(out, out_hbm, store.at[0])
    save_out.start()

    def spread_tile(t):
        sums[t + 1] = sums[link(1, t)] + transposed_dot(tiles[t], gagg[rows_s[t]])

    def spread(first, last):
        @pl.loop(first // STEP, last // STEP)
        def _(g):
            for u in range(STEP):
                spread_tile(STEP * g + u)

    spread(NEAR, TILES)
    for b in range(8):
        rows = sums[link(1, TILES + 20 + b)]
        back_out[pl.ds(16 * b, 16)] = rows.reshape(16, SLOTS, F).astype(BF16)
    landing = back_in.at[quarter, me // 4]
    pltpu.make_async_copy(back_out.at[me], landing, recv.at[BACK]).start()

    @pl.loop(1, N)
    def _(i):
        step = lax.rem(i * 91, N)
        there = moved(step // 32, lax.rem(step // 8, 4), lax.rem(step // 2, 4))
        peer = 2 * there + lax.rem(core + step, 2)
        remote(back_out.at[peer], landing, BACK, peer).start()

    term[...] = jnp.zeros_like(term)

    @pl.loop(0, 4)
    def _(k):
        here = pl.ds(pl.multiple_of(k * 512, 512), 512)
        agg = near[pl.ds(4 * k, 4)].reshape(512, F)
        term[...] += transposed_dot(agg, cot[here, :])

    whole = (term[...] * (1.0 / 512.0)).reshape(CHIPS, 8, F).astype(BF16)
    term_out[0] = whole[:, :, :HALF]
    term_out[1] = whole[:, :, HALF:]
    pair = remote(term_out.at[other], term_got, TERM_PAIR, sibling)
    pair.start()
    spread(0, 32)
    pair.wait()
    term_half[...] = (term_out[core].astype(F32) + term_got[...].astype(F32)).astype(BF16)
    pltpu.make_async_copy(term_half.at[chip], term_in.at[chip], recv.at[TERM]).start()
    to_plane(lambda there: term_half.at[there], term_in.at[chip], TERM)
    spread(32, NEAR)

    for b in range(4):
        rows = sums[link(1, TILES + 16 + b)].reshape(16, 8, F).astype(BF16)
        term_out[0, pl.ds(16 * b, 16)] = rows[:, :, :HALF]
        term_out[1, pl.ds(16 * b, 16)] = rows[:, :, HALF:]
    pair = remote(term_out.at[other], hub_back_got, BACK_PAIR, sibling)
    pair.start()
    pair.wait()
    hub_back_half[...] = (
        term_out[core].astype(F32) + hub_back_got[...].astype(F32)
    ).astype(BF16)
    pltpu.make_async_copy(hub_back_half.at[chip], hub_back.at[chip], recv.at[HUB_BACK]).start()
    to_plane(lambda there: hub_back_half.at[there], hub_back.at[chip], HUB_BACK)

    whole_wait(term_in, recv.at[TERM])
    share[0] = jnp.sum(term_in[...].astype(F32), axis=0).astype(BF16)
    pltpu.make_async_copy(share.at[0], gathered.at[core, chip], recv.at[SHARE]).start()
    to_plane(lambda there: share.at[0], gathered.at[core, chip], SHARE)

    whole_wait(back_in, recv.at[BACK])

    @pl.loop(0, 8)
    def _(k):
        here = pl.ds(pl.multiple_of(k * HALF, HALF), HALF)
        back = jnp.dot(
            picks[here, :], back_in[...].reshape(N * SLOTS, F), preferred_element_type=F32
        )
        for j in range(2):
            at = link(1, TILES + 2 * k + j)
            sums[2 * k + j + MORE] = sums[at] + back[j * TILE : j * TILE + TILE]

    whole_wait(hub_back, recv.at[HUB_BACK])
    hub_pair[0] = jnp.sum(hub_back[...].astype(F32), axis=0)
    pair = remote(hub_pair.at[0], hub_pair.at[1], LAST_PAIR, sibling)
    pair.start()
    hub_rows[...] = jnp.zeros_like(hub_rows)
    save_out.wait()
    pair.wait()
    first = jnp.where(core == 0, hub_pair[0], hub_pair[1])
    second = jnp.where(core == 0, hub_pair[1], hub_pair[0])
    total = jnp.concatenate([first, second], axis=1)
    upper = total.astype(BF16).astype(F32)
    hub_rows[pl.ds(0, 16), :] = jnp.concatenate([upper, total - upper], axis=0).astype(BF16)

    @pl.loop(0, 8)
    def _(k):
        here = pl.ds(pl.multiple_of(k * HALF, HALF), HALF)
        hub = jnp.dot(hub_picks[here, :], hub_rows[...], preferred_element_type=F32)
        mine = sums[pl.ds(2 * k + MORE, 2)].reshape(HALF, F)
        out[here, :] = (mine + hub).astype(BF16)

    save_grad = pltpu.make_async_copy(out, gfeat_hbm, store.at[0])
    save_grad.start()
    whole_wait(gathered.at[core], recv.at[SHARE])
    pair = remote(gathered.at[core], gathered.at[core], SHARE_PAIR, sibling)
    pair.start()
    pair.wait()
    save_weight = pltpu.make_async_copy(gathered, gweight_hbm, store.at[1])
    save_weight.start()
    whole_wait(hub_back.at[pl.ds(0, CHIPS - 1)], send.at[HUB])
    whole_wait(halo_in.at[pl.ds(0, N - 1)], send.at[HALO])
    whole_wait(hub_back.at[pl.ds(0, CHIPS - 1)], send.at[TERM])
    whole_wait(halo_in.at[pl.ds(0, N - 1)], send.at[BACK])
    whole_wait(hub_back.at[pl.ds(0, CHIPS - 1)], send.at[HUB_BACK])
    whole_wait(hub_back.at[pl.ds(0, CHIPS - 1)], send.at[SHARE])
    save_grad.wait()
    save_weight.wait()


def finish(
    out_in, gfeat_in, gathered_hbm, out_ref, gfeat_ref, gweight_hbm, staged, gathered, gweight, come, go
):
    last = (
        pltpu.make_async_copy(gathered_hbm, gathered, come.at[8]),
        pltpu.make_async_copy(gweight, gweight_hbm, go.at[8]),
    )
    last[0].start()
    pairs = []
    for a, (src, dst) in enumerate(((out_in, out_ref), (gfeat_in, gfeat_ref))):
        for b in range(4):
            here, slot = pl.ds(b * 512, 512), 4 * a + b
            pairs.append((
                pltpu.make_async_copy(src.at[here], staged.at[slot], come.at[slot]),
                pltpu.make_async_copy(staged.at[slot], dst.at[here], go.at[slot]),
            ))
    for first, _ in pairs:
        first.start()
    last[0].wait()
    for q in range(2):
        gweight[:, :, q * HALF : q * HALF + HALF] = gathered[q].astype(F32)
    last[1].start()
    for first, second in pairs:
        first.wait()
        second.start()
    for _, second in pairs:
        second.wait()
    last[1].wait()


def per_device(
    features, weight, cotangent, tile_values, tile_rows, tile_cols, hub_rows, send_rows, send_count
):
    smem = pl.BlockSpec(memory_space=pltpu.SMEM)
    vmem = pl.BlockSpec(memory_space=pltpu.VMEM)
    anywhere = pl.BlockSpec(memory_space=pl.ANY)
    plane = (2, CHIPS, 8, HALF)
    output, grad_features, gathered = pl.pallas_call(
        body,
        out_shape=(
            jax.ShapeDtypeStruct((R, F), BF16),
            jax.ShapeDtypeStruct((R, F), BF16),
            jax.ShapeDtypeStruct(plane, BF16),
        ),
        in_specs=[smem] * 3 + [vmem] * 4 + [anywhere, vmem, anywhere, anywhere],
        out_specs=(anywhere,) * 3,
        scratch_shapes=[
            pltpu.VMEM((TILES, TILE, TILE), BF16),
            pltpu.VMEM((20, TILE, F), BF16),
            pltpu.VMEM((8, TILE, F), BF16),
            pltpu.VMEM((R, F), BF16),
            pltpu.VMEM((R, F), BF16),
            pltpu.VMEM((MORE + 16, TILE, F), F32),
            pltpu.VMEM((16, TILE, F), BF16),
            pltpu.VMEM((F, F), F32),
            pltpu.VMEM((TILE, TILE), F32),
            pltpu.VMEM((N * SLOTS, TILE), jnp.int32),
            pltpu.VMEM((R, N * SLOTS), BF16),
            pltpu.VMEM((R, TILE), BF16),
            pltpu.VMEM((8, TILE), jnp.int32),
            pltpu.VMEM((8, TILE), jnp.int32),
            pltpu.VMEM((2, 8, HALF), BF16),
            pltpu.VMEM((1, 8, HALF), BF16),
            pltpu.VMEM((1, 8, HALF), BF16),
            pltpu.VMEM(plane, BF16),
            pltpu.VMEM((4, 32, SLOTS, F), BF16),
            pltpu.VMEM((N, SLOTS, F), BF16),
            pltpu.VMEM(plane, BF16),
            pltpu.VMEM(plane[1:], BF16),
            pltpu.VMEM(plane[1:], BF16),
            pltpu.VMEM(plane[1:], BF16),
            pltpu.VMEM((1, 8, HALF), BF16),
            pltpu.VMEM(plane, BF16),
            pltpu.VMEM((N, SLOTS, F), BF16),
            pltpu.VMEM((4, 32, SLOTS, F), BF16),
            pltpu.VMEM(plane[1:], BF16),
            pltpu.VMEM(plane[1:], BF16),
            pltpu.VMEM(plane[1:], BF16),
            pltpu.VMEM((2, 8, HALF), F32),
            pltpu.VMEM((TILE, F), BF16),
            pltpu.SMEM((8, TILE), jnp.int32),
            pltpu.SemaphoreType.DMA((4,)),
            pltpu.SemaphoreType.DMA((2,)),
            pltpu.SemaphoreType.DMA((12,)),
            pltpu.SemaphoreType.DMA((12,)),
        ],
        compiler_params=pltpu.CompilerParams(
            collective_id=0, has_side_effects=True, vmem_limit_bytes=LIMIT
        ),
        name="graph_layer",
    )(
        tile_rows, tile_cols, hub_rows, tile_rows.reshape(1, TILES), tile_cols.reshape(1, TILES),
        send_rows[0].T, send_count, features.reshape(16, TILE, F), weight, cotangent, tile_values,
    )
    output, grad_features, grad_weight = pl.pallas_call(
        finish,
        out_shape=(
            jax.ShapeDtypeStruct((R, F), BF16),
            jax.ShapeDtypeStruct((R, F), BF16),
            jax.ShapeDtypeStruct((CHIPS, 8, F), F32),
        ),
        in_specs=[anywhere] * 3,
        out_specs=(anywhere,) * 3,
        scratch_shapes=[
            pltpu.VMEM((8, 512, F), BF16),
            pltpu.VMEM(plane, BF16),
            pltpu.VMEM((CHIPS, 8, F), F32),
            pltpu.SemaphoreType.DMA((9,)),
            pltpu.SemaphoreType.DMA((9,)),
        ],
        name="finish",
    )(output, grad_features, gathered)
    return output, grad_features, grad_weight.reshape(F, F)


def solution(mesh):
    placed = (
        P("dom", None),
        P(),
        P("dom", None),
        P("dom", None, None),
        P("dom"),
        P("dom"),
        P("dom"),
        P("dom", None, None),
        P("dom", None),
    )
    return jax.shard_map(
        per_device,
        mesh=mesh,
        in_specs=placed,
        out_specs=(P("dom", None), P("dom", None), P()),
        check_vma=False,
    )
```

```python
import jax
import jax.numpy as jnp
from jax import lax
from jax.experimental import pallas as pl
from jax.experimental.pallas import tpu as pltpu
from jax.sharding import PartitionSpec as P

MESH = pl.DeviceIdType.MESH
N = 128
CHIPS = 64
F = 512
HALF = 256
R = 2048
TILE = 128
SLOTS = 8
HUBS = 4
TILES = 96
NEAR = 64
F32 = jnp.float32
BF16 = jnp.bfloat16
LIMIT = 62 * 1024 * 1024
STEP = 8
(
    PAIR, HUB, HUB_SHARE, HALO, TERM_PAIR, TERM, BACK, BACK_PAIR, HUB_BACK, SHARE, SHARE_PAIR,
    LAST_PAIR,
) = range(12)
MORE = TILES + 1


def whole_wait(ref, sem):
    pltpu.make_async_copy(ref, ref, sem).wait()


def one_hot(index, lanes):
    return (index == lanes).astype(F32).astype(BF16)


def transposed_dot(a, b):
    return lax.dot_general(a, b, (((0,), (0,)), ((), ())), preferred_element_type=F32)


def body(
    rows_s, cols_s, hub_s, rows_ref, cols_ref, send_ref, count_ref, feat_hbm, weight_ref, cot_hbm,
    tiles_hbm,
    out_hbm, gfeat_hbm, gweight_hbm,
    tiles, near, far, cot, out, sums, gagg, term, turned, column, picks, hub_picks, ids, links_v,
    hub_own, hub_got, hub_half, hub_in, halo_out, halo_in,
    term_out, term_got, term_half, term_in, share, gathered, back_out, back_in,
    hub_back_got, hub_back_half, hub_back, hub_pair, hub_rows,
    links, load, store, send, recv,
):
    me = lax.axis_index("dom")
    chip, core = me // 2, lax.rem(me, 2)
    sibling = me + 1 - 2 * core
    other = 1 - core

    loads = (
        pltpu.make_async_copy(feat_hbm, near.at[pl.ds(0, 16)], load.at[0]),
        pltpu.make_async_copy(tiles_hbm, tiles, load.at[1]),
        pltpu.make_async_copy(cot_hbm, cot, load.at[2]),
    )
    for copy in loads:
        copy.start()

    barrier = pltpu.get_barrier_semaphore()

    @pl.loop(1, N)
    def _(i):
        pl.semaphore_signal(
            barrier, inc=1, device_id=(lax.rem(me + i, N),), device_id_type=MESH
        )

    def remote(src, dst, slot, peer):
        return pltpu.make_async_remote_copy(
            src_ref=src, dst_ref=dst, send_sem=send.at[slot], recv_sem=recv.at[slot],
            device_id=(peer,), device_id_type=MESH,
        )

    def link(q, t):
        return jnp.clip(links[q, t], 0, TILES)

    at_x, at_z, at_y = chip // 16, lax.rem(chip // 4, 4), lax.rem(chip, 4)

    def moved(dx, dz, dy):
        return (
            lax.rem(at_x + dx, 4) * 16 + lax.rem(at_z + dz, 4) * 4 + lax.rem(at_y + dy, 4)
        )

    def to_plane(source, target, slot):
        @pl.loop(1, CHIPS)
        def _(j):
            step = lax.rem(j * 43, CHIPS)
            there = moved(step // 16, lax.rem(step // 4, 4), lax.rem(step, 4))
            remote(source(there), target, slot, 2 * there + core).start()

    slot_iota = lax.broadcasted_iota(jnp.int32, (SLOTS, N), 0)
    index = jnp.where(slot_iota < count_ref[...], send_ref[...], -1).astype(F32)
    turned[...] = jnp.concatenate([index, jnp.zeros((N - SLOTS, N), F32)], axis=0).T
    sub = lax.broadcasted_iota(jnp.int32, (TILE, TILE), 0)
    lane = lax.broadcasted_iota(jnp.int32, (TILE, TILE), 1)
    diagonal = lax.broadcasted_iota(jnp.int32, (HALF, TILE), 1) == lax.rem(
        lax.broadcasted_iota(jnp.int32, (HALF, TILE), 0), SLOTS
    )
    for b in range(4):
        part = turned[pl.ds(b, 32, stride=4), :]
        spread = jnp.broadcast_to(part[:, None, :], (32, SLOTS, N)).reshape(HALF, TILE)
        one = jnp.sum(jnp.where(diagonal, spread, 0.0), axis=1, keepdims=True)
        column[pl.ds(b * HALF, HALF), :] = jnp.broadcast_to(one, (HALF, TILE)).astype(jnp.int32)

    hub_at = lax.broadcasted_iota(jnp.int32, (8, R), 0)
    hub_id = jnp.full((8, R), -1, jnp.int32)
    for j in range(HUBS):
        hub_id = jnp.where(hub_at == HUBS * core + j, hub_s[j], hub_id)

    loads[0].wait()
    lanes = lax.broadcasted_iota(jnp.int32, (8, R), 1)
    rows = jnp.dot(
        one_hot(hub_id, lanes), near[pl.ds(0, 16)].reshape(R, F), preferred_element_type=F32
    ).astype(BF16)
    hub_own[0] = rows[:, :HALF]
    hub_own[1] = rows[:, HALF:]

    def gather(block):
        here = column[pl.ds(pl.multiple_of(block * HALF, HALF), HALF), 0:1]
        rows = jnp.dot(
            one_hot(here, lax.broadcasted_iota(jnp.int32, (HALF, R), 1)),
            near[pl.ds(0, 16)].reshape(R, F), preferred_element_type=F32,
        )
        halo_out[block] = rows.reshape(32, SLOTS, F).astype(BF16)

    quarter = lax.rem(me, 4)

    def block_of(b):
        return 2 * lax.rem(at_y + b // 2, 2) + lax.rem(core + b, 2)

    def send_block(b):
        block = block_of(b)

        @pl.loop(1 if b == 0 else 0, 32)
        def _(j):
            step = lax.rem(j * 11, 32)
            there = moved(step // 8, lax.rem(step // 2, 4), 2 * lax.rem(step, 2) + b // 2)
            peer = 2 * there + lax.rem(block, 2)
            remote(halo_out.at[block, peer // 4], halo_in.at[me], HALO, peer).start()

    gather(quarter)
    pl.semaphore_wait(barrier, N - 1)
    pair = remote(hub_own.at[other], hub_got.at[0], PAIR, sibling)
    pair.start()
    pltpu.make_async_copy(halo_out.at[quarter, me // 4], halo_in.at[me], recv.at[HALO]).start()
    send_block(0)
    gather(block_of(1))
    pair.wait()
    hub_half[0] = hub_own[core] + hub_got[0]
    pltpu.make_async_copy(hub_half.at[0], hub_in.at[core, chip], recv.at[HUB]).start()
    to_plane(lambda there: hub_half.at[0], hub_in.at[core, chip], HUB)
    send_block(1)
    for b in range(2, 4):
        gather(block_of(b))
        send_block(b)

    ids[...] = jnp.zeros_like(ids)
    ids[0:1, 0:TILES] = rows_ref[...]
    ids[1:2, 0:TILES] = cols_ref[...]
    links_v[...] = jnp.zeros_like(links_v)
    for q in range(2):
        keys = jnp.broadcast_to(ids[q : q + 1, :], (TILE, TILE))
        asked = jnp.where(lane < TILES, keys, lane - TILES)
        before = (keys.T == asked) & (sub < jnp.minimum(lane, TILES))
        number = jnp.where(before, sub + 1, 0)
        links_v[q : q + 1, :] = jnp.max(number, axis=0, keepdims=True)
    copy_links = pltpu.make_async_copy(links_v, links, load.at[3])
    copy_links.start()
    sums[0] = jnp.zeros((TILE, F), F32)

    for b in range(8):
        picks_row = column[pl.ds(b * TILE, TILE), :].astype(F32).T.astype(jnp.int32)[0:1, :]

        @pl.loop(0, 16)
        def _(k):
            here = pl.ds(pl.multiple_of(k * TILE, TILE), TILE)
            picks[here, pl.ds(b * TILE, TILE)] = one_hot(picks_row, sub + k * TILE)

    hub_lane = lax.rem(lane, 8)
    hub_row = jnp.full((TILE, TILE), -1, jnp.int32)
    for j in range(HUBS):
        hub_row = jnp.where((hub_lane == HUBS * core + j) & (lane < 16), hub_s[j], hub_row)

    @pl.loop(0, 16)
    def _(k):
        here = pl.ds(pl.multiple_of(k * TILE, TILE), TILE)
        hub_picks[here, :] = one_hot(hub_row, sub + k * TILE)

    whole_wait(hub_in.at[core], recv.at[HUB])
    pair = remote(hub_in.at[core], hub_in.at[core], HUB_SHARE, sibling)
    pair.start()
    loads[1].wait()
    copy_links.wait()
    pair.wait()
    for b in range(4):
        for q in range(2):
            near[16 + b, :, q * HALF : q * HALF + HALF] = hub_in[q, pl.ds(16 * b, 16)].reshape(
                TILE, HALF
            )

    @pl.loop(0, NEAR // STEP)
    def _(g):
        for u in range(STEP):
            t = STEP * g + u
            sums[t + 1] = sums[link(0, t)] + jnp.dot(
                tiles[t], near[cols_s[t]], preferred_element_type=F32
            )

    whole_wait(halo_in, recv.at[HALO])
    far[...] = halo_in[...].reshape(8, TILE, F)

    @pl.loop(0, (TILES - NEAR) // STEP)
    def _(g):
        for u in range(STEP):
            t = NEAR + STEP * g + u
            sums[t + 1] = sums[link(0, t)] + jnp.dot(
                tiles[t], far[jnp.maximum(cols_s[t] - 20, 0)], preferred_element_type=F32
            )

    loads[2].wait()
    weight = weight_ref[...]

    agg = jnp.concatenate([sums[link(0, TILES + j)] for j in range(16)], axis=0).astype(BF16)
    near[pl.ds(0, 16)] = agg.reshape(16, TILE, F)
    pre = jnp.dot(agg, weight, preferred_element_type=F32)
    sig = 0.5 * jnp.tanh(0.5 * pre) + 0.5
    out[...] = (pre * sig).astype(BF16)
    gpre = (cot[...].astype(F32) * sig * (1.0 + pre * (1.0 - sig))).astype(BF16)
    cot[...] = gpre
    back = lax.dot_general(gpre, weight, (((1,), (1,)), ((), ())), preferred_element_type=F32)
    gagg[...] = back.astype(BF16).reshape(16, TILE, F)

    save_out = pltpu.make_async_copy(out, out_hbm, store.at[0])
    save_out.start()

    def spread_tile(t):
        sums[t + 1] = sums[link(1, t)] + transposed_dot(tiles[t], gagg[rows_s[t]])

    def spread(first, last):
        @pl.loop(first // STEP, last // STEP)
        def _(g):
            for u in range(STEP):
                spread_tile(STEP * g + u)

    term[...] = jnp.zeros_like(term)

    @pl.loop(0, 4)
    def _(k):
        here = pl.ds(pl.multiple_of(k * 512, 512), 512)
        agg = near[pl.ds(4 * k, 4)].reshape(512, F)
        term[...] += transposed_dot(agg, cot[here, :])

    whole = (term[...] * (1.0 / 512.0)).reshape(CHIPS, 8, F).astype(BF16)
    term_out[0] = whole[:, :, :HALF]
    term_out[1] = whole[:, :, HALF:]
    pair = remote(term_out.at[other], term_got, TERM_PAIR, sibling)
    pair.start()
    spread(NEAR, TILES)
    pair.wait()
    term_half[...] = (term_out[core].astype(F32) + term_got[...].astype(F32)).astype(BF16)
    pltpu.make_async_copy(term_half.at[chip], term_in.at[chip], recv.at[TERM]).start()
    to_plane(lambda there: term_half.at[there], term_in.at[chip], TERM)
    for b in range(8):
        rows = sums[link(1, TILES + 20 + b)]
        back_out[pl.ds(16 * b, 16)] = rows.reshape(16, SLOTS, F).astype(BF16)
    landing = back_in.at[quarter, me // 4]
    pltpu.make_async_copy(back_out.at[me], landing, recv.at[BACK]).start()

    @pl.loop(1, N)
    def _(i):
        peer = lax.rem(me + 37 * i, N)
        remote(back_out.at[peer], landing, BACK, peer).start()

    spread(0, 32)
    spread(32, NEAR)

    for b in range(4):
        rows = sums[link(1, TILES + 16 + b)].reshape(16, 8, F).astype(BF16)
        term_out[0, pl.ds(16 * b, 16)] = rows[:, :, :HALF]
        term_out[1, pl.ds(16 * b, 16)] = rows[:, :, HALF:]
    pair = remote(term_out.at[other], hub_back_got, BACK_PAIR, sibling)
    pair.start()
    pair.wait()
    hub_back_half[...] = (
        term_out[core].astype(F32) + hub_back_got[...].astype(F32)
    ).astype(BF16)
    pltpu.make_async_copy(hub_back_half.at[chip], hub_back.at[chip], recv.at[HUB_BACK]).start()
    to_plane(lambda there: hub_back_half.at[there], hub_back.at[chip], HUB_BACK)

    whole_wait(term_in, recv.at[TERM])
    share[0] = jnp.sum(term_in[...].astype(F32), axis=0).astype(BF16)
    pltpu.make_async_copy(share.at[0], gathered.at[core, chip], recv.at[SHARE]).start()
    to_plane(lambda there: share.at[0], gathered.at[core, chip], SHARE)

    whole_wait(back_in, recv.at[BACK])

    @pl.loop(0, 8)
    def _(k):
        here = pl.ds(pl.multiple_of(k * HALF, HALF), HALF)
        back = jnp.dot(
            picks[here, :], back_in[...].reshape(N * SLOTS, F), preferred_element_type=F32
        )
        for j in range(2):
            at = link(1, TILES + 2 * k + j)
            sums[2 * k + j + MORE] = sums[at] + back[j * TILE : j * TILE + TILE]

    whole_wait(hub_back, recv.at[HUB_BACK])
    hub_pair[0] = jnp.sum(hub_back[...].astype(F32), axis=0)
    pair = remote(hub_pair.at[0], hub_pair.at[1], LAST_PAIR, sibling)
    pair.start()
    hub_rows[...] = jnp.zeros_like(hub_rows)
    save_out.wait()
    pair.wait()
    first = jnp.where(core == 0, hub_pair[0], hub_pair[1])
    second = jnp.where(core == 0, hub_pair[1], hub_pair[0])
    total = jnp.concatenate([first, second], axis=1)
    upper = total.astype(BF16).astype(F32)
    hub_rows[pl.ds(0, 16), :] = jnp.concatenate([upper, total - upper], axis=0).astype(BF16)

    saves = []
    for k in range(4):
        here = pl.ds(k * 512, 512)
        hub = jnp.dot(hub_picks[here, :], hub_rows[...], preferred_element_type=F32)
        mine = sums[pl.ds(4 * k + MORE, 4)].reshape(512, F)
        out[here, :] = (mine + hub).astype(BF16)
        saves.append(pltpu.make_async_copy(out.at[here], gfeat_hbm.at[here], store.at[2 + k]))
        saves[k].start()

    whole_wait(gathered.at[core], recv.at[SHARE])
    pair = remote(gathered.at[core], gathered.at[core], SHARE_PAIR, sibling)
    pair.start()
    pair.wait()
    save_weight = pltpu.make_async_copy(gathered, gweight_hbm, store.at[1])
    save_weight.start()
    whole_wait(hub_back.at[pl.ds(0, CHIPS - 1)], send.at[HUB])
    whole_wait(halo_in.at[pl.ds(0, N - 1)], send.at[HALO])
    whole_wait(hub_back.at[pl.ds(0, CHIPS - 1)], send.at[TERM])
    whole_wait(halo_in.at[pl.ds(0, N - 1)], send.at[BACK])
    whole_wait(hub_back.at[pl.ds(0, CHIPS - 1)], send.at[HUB_BACK])
    whole_wait(hub_back.at[pl.ds(0, CHIPS - 1)], send.at[SHARE])
    for copy in saves:
        copy.wait()
    save_weight.wait()


def finish(
    out_in, gfeat_in, gathered_hbm, out_ref, gfeat_ref, gweight_hbm, staged, gathered, gweight, come, go
):
    last = (
        pltpu.make_async_copy(gathered_hbm, gathered, come.at[8]),
        pltpu.make_async_copy(gweight, gweight_hbm, go.at[8]),
    )
    last[0].start()
    pairs = []
    for a, (src, dst) in enumerate(((out_in, out_ref), (gfeat_in, gfeat_ref))):
        for b in range(4):
            here, slot = pl.ds(b * 512, 512), 4 * a + b
            pairs.append((
                pltpu.make_async_copy(src.at[here], staged.at[slot], come.at[slot]),
                pltpu.make_async_copy(staged.at[slot], dst.at[here], go.at[slot]),
            ))
    for first, _ in pairs:
        first.start()
    last[0].wait()
    for q in range(2):
        gweight[:, :, q * HALF : q * HALF + HALF] = gathered[q].astype(F32)
    last[1].start()
    for first, second in pairs:
        first.wait()
        second.start()
    for _, second in pairs:
        second.wait()
    last[1].wait()


def per_device(
    features, weight, cotangent, tile_values, tile_rows, tile_cols, hub_rows, send_rows, send_count
):
    smem = pl.BlockSpec(memory_space=pltpu.SMEM)
    vmem = pl.BlockSpec(memory_space=pltpu.VMEM)
    anywhere = pl.BlockSpec(memory_space=pl.ANY)
    plane = (2, CHIPS, 8, HALF)
    output, grad_features, gathered = pl.pallas_call(
        body,
        out_shape=(
            jax.ShapeDtypeStruct((R, F), BF16),
            jax.ShapeDtypeStruct((R, F), BF16),
            jax.ShapeDtypeStruct(plane, BF16),
        ),
        in_specs=[smem] * 3 + [vmem] * 4 + [anywhere, vmem, anywhere, anywhere],
        out_specs=(anywhere,) * 3,
        scratch_shapes=[
            pltpu.VMEM((TILES, TILE, TILE), BF16),
            pltpu.VMEM((20, TILE, F), BF16),
            pltpu.VMEM((8, TILE, F), BF16),
            pltpu.VMEM((R, F), BF16),
            pltpu.VMEM((R, F), BF16),
            pltpu.VMEM((MORE + 16, TILE, F), F32),
            pltpu.VMEM((16, TILE, F), BF16),
            pltpu.VMEM((F, F), F32),
            pltpu.VMEM((TILE, TILE), F32),
            pltpu.VMEM((N * SLOTS, TILE), jnp.int32),
            pltpu.VMEM((R, N * SLOTS), BF16),
            pltpu.VMEM((R, TILE), BF16),
            pltpu.VMEM((8, TILE), jnp.int32),
            pltpu.VMEM((8, TILE), jnp.int32),
            pltpu.VMEM((2, 8, HALF), BF16),
            pltpu.VMEM((1, 8, HALF), BF16),
            pltpu.VMEM((1, 8, HALF), BF16),
            pltpu.VMEM(plane, BF16),
            pltpu.VMEM((4, 32, SLOTS, F), BF16),
            pltpu.VMEM((N, SLOTS, F), BF16),
            pltpu.VMEM(plane, BF16),
            pltpu.VMEM(plane[1:], BF16),
            pltpu.VMEM(plane[1:], BF16),
            pltpu.VMEM(plane[1:], BF16),
            pltpu.VMEM((1, 8, HALF), BF16),
            pltpu.VMEM(plane, BF16),
            pltpu.VMEM((N, SLOTS, F), BF16),
            pltpu.VMEM((4, 32, SLOTS, F), BF16),
            pltpu.VMEM(plane[1:], BF16),
            pltpu.VMEM(plane[1:], BF16),
            pltpu.VMEM(plane[1:], BF16),
            pltpu.VMEM((2, 8, HALF), F32),
            pltpu.VMEM((TILE, F), BF16),
            pltpu.SMEM((8, TILE), jnp.int32),
            pltpu.SemaphoreType.DMA((4,)),
            pltpu.SemaphoreType.DMA((6,)),
            pltpu.SemaphoreType.DMA((12,)),
            pltpu.SemaphoreType.DMA((12,)),
        ],
        compiler_params=pltpu.CompilerParams(
            collective_id=0, has_side_effects=True, vmem_limit_bytes=LIMIT
        ),
        name="graph_layer",
    )(
        tile_rows, tile_cols, hub_rows, tile_rows.reshape(1, TILES), tile_cols.reshape(1, TILES),
        send_rows[0].T, send_count, features.reshape(16, TILE, F), weight, cotangent, tile_values,
    )
    output, grad_features, grad_weight = pl.pallas_call(
        finish,
        out_shape=(
            jax.ShapeDtypeStruct((R, F), BF16),
            jax.ShapeDtypeStruct((R, F), BF16),
            jax.ShapeDtypeStruct((CHIPS, 8, F), F32),
        ),
        in_specs=[anywhere] * 3,
        out_specs=(anywhere,) * 3,
        scratch_shapes=[
            pltpu.VMEM((8, 512, F), BF16),
            pltpu.VMEM(plane, BF16),
            pltpu.VMEM((CHIPS, 8, F), F32),
            pltpu.SemaphoreType.DMA((9,)),
            pltpu.SemaphoreType.DMA((9,)),
        ],
        name="finish",
    )(output, grad_features, gathered)
    return output, grad_features, grad_weight.reshape(F, F)


def solution(mesh):
    placed = (
        P("dom", None),
        P(),
        P("dom", None),
        P("dom", None, None),
        P("dom"),
        P("dom"),
        P("dom"),
        P("dom", None, None),
        P("dom", None),
    )
    return jax.shard_map(
        per_device,
        mesh=mesh,
        in_specs=placed,
        out_specs=(P("dom", None), P("dom", None), P()),
        check_vma=False,
    )
```
